32 devices in a mesh: row: 8 (over z, core), col: 4 (over y, x).
Axes of the slice: x: 2, y: 2, z: 4, core: 2. Of those that a mesh axis runs over, the one named last changes fastest.
Arguments:
- tokens: bfloat16 [16384, 1024], P(('row', 'col')), may hold values from -64 to 64, as said below
- merge_map: int32 [16384], P(('row', 'col')), may hold values from 0 to 511, as said below
- block_owner: int32 [32, 8], P(('row', 'col')), may hold values from -1 to 15, as said below
- neighbours: int32 [64, 4], P(('row', 'col')), may hold values from 0 to 7, as said below
- w_query: bfloat16 [1024, 512], replicated, may hold values from -0.1875 to 0.1875
- w_key: bfloat16 [1024, 512], replicated, may hold values from -0.1875 to 0.1875
- w_value: bfloat16 [1024, 512], replicated, may hold values from -0.1875 to 0.1875
Outputs:
- attended: bfloat16 [16384, 512], P(('row', 'col'))
The draws below stay inside these ranges and needn't reach their ends.
Inputs may be any that keep to these rules, and one draw needn't show every extreme that they name: `merge_map`: within a tile, the slots of its live blocks (those whose block_owner is not -1) are each used by one or more tokens, and no other slot is used. `block_owner`: A tile's live blocks are its first ones, 1 to 8 of them, 8 in some tile of every column index; a code o names owned block o % 2 of the device with row index o // 2 and the tile's column index; within one column index every code is named exactly once; one tile names each row index at most once. `neighbours`: the entries of a row are distinct, and the first is the block's own candidate number. `tokens`: finite bfloat16 values.
All inputs are finite; a program needn't handle non-finite values.
Results may differ from the reference program's by a relative error of at most 0.019.
The reference program's roundings to bfloat16 on the way count: a program that leaves them out, or rounds other values in their place, can miss the bound.
Values may be sent and summed in bfloat16 or wider, within the bound.
No kernel may reach another device: no remote copies, remote signals or barrier semaphores. Data moves between devices by JAX's collectives and lax.ppermute only.
A program may use at most 64 MiB of HBM per device.

```python
import math
import jax
import jax.numpy as jnp
from jax import lax

D = 1024
HEADS = 8
HD = 64
BLK = 64
OWN = 2
SLOTS_BLK = 8
TOK_DEV = 512
TOKENS = 16384
BLOCKS = 64
NB = 4
N_ROW = 8
N_COL = 4


def live_blocks(key):
    pattern = jnp.array([8, 2, 1, 1, 1, 1, 1, 1], jnp.int32)
    row_kind = pattern[jnp.arange(N_ROW, dtype=jnp.int32) % 8]
    col_keys = jax.random.split(jax.random.fold_in(key, 11), N_COL)

    def column(col_key):
        shuffled = jax.random.permutation(col_key, N_ROW)
        return row_kind[shuffled]
    per_col = jax.vmap(column)(col_keys)
    return per_col.T.reshape(-1)


def draw_block_owner(key, part):
    live_count = live_blocks(key).reshape(N_ROW, N_COL)
    row_start = jnp.cumsum(live_count, axis=0) - live_count
    block_ids = jnp.arange(SLOTS_BLK, dtype=jnp.int32)
    ranked = row_start[:, :, None] + block_ids[None, None, :]
    dest_code = ranked % N_ROW * OWN + ranked // N_ROW
    result = jnp.where(block_ids[None, None, :] < live_count[:, :, None], dest_code, -1)
    return result.reshape(N_ROW * N_COL, SLOTS_BLK).astype(jnp.int32)


def draw_merge_map(key, part):
    live_count = live_blocks(key)
    used_slots = live_count * BLK
    tile_keys = jax.random.split(jax.random.fold_in(key, 23), N_ROW * N_COL)

    def tile(tile_key, used):
        first_key, second_key = jax.random.split(tile_key)
        shuffled = jax.random.permutation(first_key, TOK_DEV)
        position = jnp.argsort(shuffled).astype(jnp.int32)
        spare_slot = jax.random.randint(second_key, (TOK_DEV,), 0, used)
        return jnp.where(position < used, position, spare_slot)
    return jax.vmap(tile)(tile_keys, used_slots).reshape(-1).astype(jnp.int32)


def draw_neighbours(key, part):
    cand_total = N_COL * OWN
    block_keys = jax.random.split(jax.random.fold_in(key, 37), BLOCKS)
    block_ids = jnp.arange(BLOCKS, dtype=jnp.int32)
    self_ids = block_ids // OWN % N_COL * OWN + block_ids % OWN

    def listing(block_key, self_id):
        shuffled = jax.random.permutation(block_key, cand_total)
        rank_key = jnp.where(shuffled == self_id, -1, jnp.arange(cand_total, dtype=jnp.int32))
        return shuffled[jnp.argsort(rank_key)][:NB]
    return jax.vmap(listing)(block_keys, self_ids).astype(jnp.int32)


def draw_tokens(key, part):
    normals = jax.random.truncated_normal(key, -4.0, 4.0, (TOKENS, D), jnp.float32)
    return normals.astype(jnp.bfloat16)


def normal_values(stream_key, extent, deviation, limit, kind=jnp.bfloat16):
    return jnp.clip(deviation * jax.random.normal(stream_key, extent, jnp.float32), -limit, limit).astype(kind)


def setup_inputs(seed: int = 0) -> dict:
    arg_keys = jax.random.split(jax.random.key(seed), 8)
    tokens = draw_tokens(jax.random.fold_in(arg_keys[7], 71), 0)
    merge_map = draw_merge_map(jax.random.fold_in(arg_keys[7], 71), 0)
    block_owner = draw_block_owner(jax.random.fold_in(arg_keys[7], 71), 0)
    neighbours = draw_neighbours(jax.random.fold_in(arg_keys[7], 71), 0)
    w_query = normal_values(arg_keys[4], (D, HEADS * HD), D ** -0.5, 0.1875)
    w_key = normal_values(arg_keys[5], (D, HEADS * HD), D ** -0.5, 0.1875)
    w_value = normal_values(arg_keys[6], (D, HEADS * HD), D ** -0.5, 0.1875)
    return dict(tokens=tokens, merge_map=merge_map, block_owner=block_owner, neighbours=neighbours, w_query=w_query, w_key=w_key, w_value=w_value)


def reference(tokens, merge_map, block_owner, neighbours, w_query, w_key, w_value):
    tile_count = N_ROW * N_COL
    slot_total = SLOTS_BLK * BLK
    head_width = HEADS * HD
    cand_total = N_COL * OWN
    tok_tiles = tokens.reshape(tile_count, TOK_DEV, D)
    map_tiles = merge_map.reshape(tile_count, TOK_DEV)

    def merge_tile(pair):
        tile_rows, mapping = pair
        onehot = (jnp.arange(slot_total, dtype=jnp.int32)[:, None] == mapping[None, :]).astype(jnp.float32)
        slot_sums = jnp.dot(onehot, tile_rows.astype(jnp.float32), precision=lax.Precision.HIGHEST)
        slot_count = lax.optimization_barrier(jnp.sum(onehot, axis=1))
        return (slot_sums / jnp.maximum(slot_count, 1.0)[:, None]).astype(jnp.bfloat16)
    merged = lax.map(merge_tile, (tok_tiles, map_tiles))
    blocks = merged.reshape(tile_count * SLOTS_BLK, BLK, D)
    tile_ids = jnp.arange(tile_count, dtype=jnp.int32)[:, None]
    target = (block_owner // OWN * N_COL + tile_ids % N_COL) * OWN + block_owner % OWN
    target = jnp.where(block_owner >= 0, target, BLOCKS).reshape(-1).astype(jnp.int32)
    owned_blocks = jnp.zeros((BLOCKS, BLK, D), jnp.bfloat16).at[target].set(blocks, mode='drop')
    score_scale = 1.0 / math.sqrt(HD)

    def attend_row(pair):
        row_blocks, cand_lists = pair
        row_tokens = row_blocks.reshape(-1, D)
        query_rows = jnp.dot(row_tokens, w_query, preferred_element_type=jnp.float32).astype(jnp.bfloat16)
        key_rows = jnp.dot(row_tokens, w_key, preferred_element_type=jnp.float32).astype(jnp.bfloat16)
        value_rows = jnp.dot(row_tokens, w_value, preferred_element_type=jnp.float32).astype(jnp.bfloat16)
        query_heads = query_rows.reshape(-1, HEADS, HD).astype(jnp.float32)
        key_heads = key_rows.reshape(-1, HEADS, HD).astype(jnp.float32)
        value_heads = value_rows.reshape(-1, HEADS, HD).astype(jnp.float32)
        scores = jnp.einsum('qhd,khd->hqk', query_heads, key_heads) * score_scale
        allowed = jnp.any(cand_lists[:, :, None] == jnp.arange(cand_total, dtype=jnp.int32)[None, None, :], axis=1)
        visible = jnp.repeat(jnp.repeat(allowed, BLK, axis=0), BLK, axis=1)[None]
        scores = jnp.where(visible, scores, -1e+30)
        row_max = lax.optimization_barrier(jnp.max(scores, axis=-1, keepdims=True))
        probs = jnp.where(visible, jnp.exp(scores - row_max), 0.0)
        weight_total = lax.optimization_barrier(jnp.sum(probs, axis=-1, keepdims=True))
        weights = probs.astype(jnp.bfloat16).astype(jnp.float32)
        head_out = jnp.einsum('hqk,khd->hqd', weights, value_heads) / weight_total
        return head_out.transpose(1, 0, 2).reshape(-1, head_width).astype(jnp.bfloat16)
    attended_rows = lax.map(attend_row, (owned_blocks.reshape(N_ROW, cand_total, BLK, D), neighbours.reshape(N_ROW, cand_total, NB)))
    attended_rows = attended_rows.reshape(-1, head_width)
    block_of = map_tiles // BLK
    dest_code = jnp.take_along_axis(block_owner, block_of, axis=1)
    token_index = ((dest_code // OWN * N_COL + tile_ids % N_COL) * OWN + dest_code % OWN) * BLK + map_tiles % BLK
    return attended_rows[token_index.reshape(-1).astype(jnp.int32)]
```

```python
import functools
import math

import jax
import jax.numpy as jnp
from jax import lax
from jax.experimental import pallas as pl
from jax.experimental.pallas import tpu as pltpu
from jax.sharding import PartitionSpec as P

HEADS = 8
HD = 64
BLK = 64
OWN = 2
CHUNKS = 1
LANES = 128


VMEM = pl.BlockSpec(memory_space=pltpu.VMEM)
SMEM = pl.BlockSpec(memory_space=pltpu.SMEM)


def partner(i, k, n, back=False):
    if n & (n - 1) == 0:
        return i ^ k
    return (i - k + n) % n if back else (i + k) % n


def rounds(x, axis, n, back=False):
    out = [x[0]]
    for k in range(1, n):
        pairs = [(i, partner(i, k, n, back)) for i in range(n)]
        out.append(lax.ppermute(x[k], axis, pairs))
    return out


def slot_of(owner_ref, row, slots):
    slot = jnp.int32(-1)
    code = jnp.int32(-1)
    for b in range(slots):
        o = owner_ref[0, b]
        hit = (o >= 0) & (o // OWN == row)
        slot = jnp.where(hit, b, slot)
        code = jnp.where(hit, o % OWN, code)
    return slot, code


def merge_kernel(n, slots, chunks, tok_ref, map_ref, owner_ref, tag_ref, *outs):
    me = lax.axis_index("row")
    rows = BLK // chunks
    toks = tok_ref.shape[0]
    mm = map_ref[...]
    for r in range(n):
        _, code = slot_of(owner_ref, r, slots)
        tag_ref[r] = jnp.full((1, LANES), code, jnp.int32)
    lane = lax.broadcasted_iota(jnp.int32, (rows, toks), 0)
    per = max(1, 256 // rows)
    for c in range(chunks):
        for k0 in range(0, n, per):
            group = range(k0, min(n, k0 + per))
            hot = []
            for k in group:
                slot, _ = slot_of(owner_ref, partner(me, k, n), slots)
                base = jnp.where(slot >= 0, slot * BLK + c * rows, -BLK)
                hot.append(mm == lane + base)
            hot = jnp.concatenate(hot, axis=0).astype(jnp.float32)
            count = jnp.sum(hot, axis=1, keepdims=True)
            sums = jnp.dot(
                hot.astype(jnp.bfloat16), tok_ref[...], preferred_element_type=jnp.float32
            )
            merged = (sums / jnp.maximum(count, 1.0)).astype(jnp.bfloat16)
            for j, k in enumerate(group):
                outs[c * n + k][...] = merged[j * rows : (j + 1) * rows]


def project_kernel(n, rows, tag_ref, wq_ref, wk_ref, wv_ref, *refs):
    blocks = refs[:n]
    q_ref, kv_ref, x_ref = refs[n:]
    me = lax.axis_index("row")
    for k in range(n):
        tag = tag_ref[partner(me, k, n, True), 0, 0]

        @pl.when(tag >= 0)
        def _():
            x_ref[pl.ds(pl.multiple_of(tag * rows, rows), rows), :] = blocks[k][...]

    x = x_ref[...]
    width = wk_ref.shape[1]

    def mul(w):
        return jnp.dot(x, w[...], preferred_element_type=jnp.float32).astype(jnp.bfloat16)

    kv_ref[:, :width] = mul(wk_ref)
    kv_ref[:, width:] = mul(wv_ref)
    q_ref[...] = mul(wq_ref)


def attend_kernel(n, n_col, chunks, tag_ref, near_ref, *refs):
    me = lax.axis_index("row")
    my_col = lax.axis_index("col")
    rows = BLK // chunks
    near = near_ref.shape[1]
    qs = refs[:chunks]
    kvs = refs[chunks : chunks * (1 + n_col)]
    outs = refs[chunks * (1 + n_col) : chunks * (1 + n_col) + n]
    kv_ref, head_ref = refs[chunks * (1 + n_col) + n :]
    width = qs[0].shape[1]
    for s in range(OWN):
        place = jnp.int32(0)
        for k in range(n_col):
            col = partner(my_col, k, n_col, True)
            for t in range(OWN):
                cand = col * OWN + t
                hit = near_ref[s, 0] == cand
                for j in range(1, near):
                    hit = hit | (near_ref[s, j] == cand)

                @pl.when(hit)
                def _(place=place):
                    for c in range(chunks):
                        at = pl.multiple_of(place * BLK + c * rows, rows)
                        kv_ref[s, pl.ds(at, rows), :] = kvs[c * n_col + k][
                            t * rows : (t + 1) * rows, :
                        ]

                place = place + jnp.where(hit, 1, 0)
    scale = 1.0 / math.sqrt(HD)
    low = lax.broadcasted_iota(jnp.int32, (BLK, LANES), 1) < HD
    zero = jnp.zeros((BLK, LANES), jnp.bfloat16)
    for s in range(OWN):
        for h in range(0, width, LANES):
            q = jnp.concatenate(
                [qs[c][s * rows : (s + 1) * rows, h : h + LANES] for c in range(chunks)], axis=0
            )
            q = jnp.concatenate([jnp.where(low, q, zero), jnp.where(low, zero, q)], axis=0)
            score = lax.dot_general(
                q,
                kv_ref[s, :, h : h + LANES],
                (((1,), (1,)), ((), ())),
                preferred_element_type=jnp.float32,
            )
            score = score * scale
            p = jnp.exp(score - jnp.max(score, axis=1, keepdims=True))
            total = jnp.sum(p, axis=1, keepdims=True)
            o = jnp.dot(
                p.astype(jnp.bfloat16),
                kv_ref[s, :, width + h : width + h + LANES],
                preferred_element_type=jnp.float32,
            )
            o = (o / total).astype(jnp.bfloat16)
            head_ref[s, :, h : h + LANES] = jnp.where(low, o[:BLK], o[BLK:])
    for k in range(n):
        tag = tag_ref[partner(me, k, n, True), 0, 0]

        @pl.when(tag >= 0)
        def _():
            outs[k][...] = head_ref[jnp.maximum(tag, 0)]

        @pl.when(tag < 0)
        def _():
            outs[k][...] = jnp.zeros_like(outs[k])


def spread_kernel(n, slots, map_ref, owner_ref, out_ref):
    me = lax.axis_index("row")
    mm = map_ref[...]
    block = mm // BLK
    target = mm % BLK
    for k in range(n):
        slot, _ = slot_of(owner_ref, partner(me, k, n), slots)
        target = target + jnp.where((block == slot) & (slot >= 0), k * BLK, 0)
    toks = mm.shape[1]
    for k0 in range(0, n * BLK, LANES):
        ids = lax.broadcasted_iota(jnp.int32, (LANES, toks), 0) + k0
        hot = (ids == target).astype(jnp.float32)
        out_ref[:, k0 : k0 + LANES] = jnp.transpose(hot).astype(jnp.bfloat16)


def return_kernel(n, spread_ref, *refs):
    blocks, out_ref, all_ref = refs[:n], refs[n], refs[n + 1]
    for k in range(n):
        all_ref[k * BLK : (k + 1) * BLK, :] = blocks[k][...]
    out_ref[...] = jnp.dot(
        spread_ref[...], all_ref[...], preferred_element_type=jnp.float32
    ).astype(out_ref.dtype)


def on_device(tokens, merge_map, block_owner, neighbours, w_query, w_key, w_value):
    n = lax.axis_size("row")
    n_col = lax.axis_size("col")
    toks, width = tokens.shape
    heads = w_query.shape[1]
    slots = block_owner.shape[1]
    near = neighbours.shape[1]
    rows = BLK // CHUNKS
    bf16 = jnp.bfloat16

    def shape(*s, dtype=bf16):
        return jax.ShapeDtypeStruct(s, dtype)

    mm = merge_map.reshape(1, toks)
    tag, *sent = pl.pallas_call(
        functools.partial(merge_kernel, n, slots, CHUNKS),
        out_shape=[shape(n, 1, LANES, dtype=jnp.int32)] + [shape(rows, width)] * (n * CHUNKS),
        in_specs=[VMEM, VMEM, SMEM],
        out_specs=[VMEM] * (1 + n * CHUNKS),
        name="merge",
    )(tokens, mm, block_owner)
    arrived = [rounds(sent[c * n : (c + 1) * n], "row", n) for c in range(CHUNKS)]
    tags = lax.all_to_all(tag, "row", split_axis=0, concat_axis=0, tiled=True)
    spread = pl.pallas_call(
        functools.partial(spread_kernel, n, slots),
        out_shape=shape(toks, n * BLK),
        in_specs=[VMEM, SMEM],
        out_specs=VMEM,
        name="spread",
    )(mm, block_owner)
    qs, kvs = [], []
    for c in range(CHUNKS):
        q, kv = pl.pallas_call(
            functools.partial(project_kernel, n, rows),
            out_shape=[shape(OWN * rows, heads), shape(OWN * rows, 2 * heads)],
            in_specs=[SMEM] + [VMEM] * (3 + n),
            out_specs=[VMEM, VMEM],
            scratch_shapes=[pltpu.VMEM((OWN * rows, width), bf16)],
            name="project",
        )(tags, w_query, w_key, w_value, *arrived[c])
        qs.append(q)
        kvs += rounds([kv] * n_col, "col", n_col)
    replies = pl.pallas_call(
        functools.partial(attend_kernel, n, n_col, CHUNKS),
        out_shape=[shape(BLK, heads)] * n,
        in_specs=[SMEM, SMEM] + [VMEM] * (CHUNKS * (1 + n_col)),
        out_specs=[VMEM] * n,
        scratch_shapes=[
            pltpu.VMEM((OWN, near * BLK, 2 * heads), bf16),
            pltpu.VMEM((OWN, BLK, heads), bf16),
        ],
        name="attend",
    )(tags, neighbours, *qs, *kvs)
    returned = rounds(replies, "row", n, True)
    return pl.pallas_call(
        functools.partial(return_kernel, n),
        out_shape=shape(toks, heads),
        in_specs=[VMEM] * (1 + n),
        out_specs=VMEM,
        scratch_shapes=[pltpu.VMEM((n * BLK, heads), bf16)],
        name="give_back",
    )(spread, *returned)


def solution(mesh):
    in_specs = (
        P(("row", "col"), None),
        P(("row", "col")),
        P(("row", "col"), None),
        P(("row", "col"), None),
        P(),
        P(),
        P(),
    )
    out_specs = P(("row", "col"), None)
    return jax.shard_map(
        on_device, mesh=mesh, in_specs=in_specs, out_specs=out_specs, check_vma=False
    )
```

```python
import functools
import math

import jax
import jax.numpy as jnp
from jax import lax
from jax.experimental import pallas as pl
from jax.experimental.pallas import tpu as pltpu
from jax.sharding import PartitionSpec as P


HD = 64
BLK = 64
OWN = 2
LANES = 128
TAG = 8


VMEM = pl.BlockSpec(memory_space=pltpu.VMEM)
SMEM = pl.BlockSpec(memory_space=pltpu.SMEM)
HBM = pl.BlockSpec(memory_space=pltpu.HBM)
PARAMS = pltpu.CompilerParams(vmem_limit_bytes=16 << 20)


def partner(i, k, n, back=False):
    if n & (n - 1) == 0:
        return i ^ k
    return (i - k + n) % n if back else (i + k) % n


def inner(i, k, n, back=False):
    m = n // 2
    side = (i >= m) * m
    return side + partner(i - side, k, m, back)


def across(i, n):
    m = n // 2
    return i + m - (i >= m) * n


def peer(i, k, n, back=False):
    m = n // 2
    return inner(i, k, n, back) if k < m else across(inner(i, k - m, n, back), n)


def order(n):
    return sorted(range(1, n), key=lambda k: (-(k.bit_length() - 1 if k > 1 else 0), k))


def rounds(x, axis, n, to):
    out = list(x)
    for k in order(len(x)):
        out[k] = lax.ppermute(x[k], axis, [(i, to(i, k, n)) for i in range(n)])
    return out


def cost(us):
    return pl.CostEstimate(
        flops=int(us * 8e8), bytes_accessed=int(us * 2e6), transcendentals=0
    )


FIRST = (0, BLK // 2)
SECOND = (BLK // 2, BLK - BLK // 2)
PARTS = (FIRST, SECOND)
MESSAGES = (
    ((True, *FIRST),),
    ((True, *SECOND), (False, *FIRST)),
    ((False, *SECOND),),
)


def slot_of(owner_ref, row, slots):
    slot = jnp.int32(-1)
    code = jnp.int32(-1)
    for b in range(slots):
        o = owner_ref[0, b]
        hit = (o >= 0) & (o // OWN == row)
        slot = jnp.where(hit, b, slot)
        code = jnp.where(hit, o % OWN, code)
    return slot, code


def merge_kernel(n, slots, messages, tok_hbm, map_hbm, owner_hbm, *refs):
    m = n // 2
    outs = refs[: m * len(messages)]
    tok_ref, map_ref, owner_ref, sems = refs[m * len(messages) :]
    copies = [
        pltpu.make_async_copy(src, dst, sems.at[i])
        for i, (src, dst) in enumerate(
            [(owner_hbm, owner_ref), (map_hbm, map_ref), (tok_hbm, tok_ref)]
        )
    ]
    for copy in copies:
        copy.start()
    me = lax.axis_index("row")
    toks, width = tok_ref.shape
    pieces = width // LANES
    copies[0].wait()
    dest = {}
    for far in sorted({part[0] for message in messages for part in message}):
        for k in range(m):
            to = inner(me, k, n)
            dest[far, k] = slot_of(owner_ref, across(to, n) if far else to, slots)
    work = []
    for i, message in enumerate(messages):
        at = 0
        for far, start, rows in message:
            work += [(i * m + k, at, dest[far, k], start, rows) for k in range(m)]
            at += rows * pieces
            if start == 0:
                end = sum(part[2] for part in message) * pieces
                for k in range(m):
                    outs[i * m + k][end:, :] = jnp.full(
                        (TAG, LANES), dest[far, k][1], jnp.int32
                    ).astype(jnp.bfloat16)
    copies[1].wait()
    mm = map_ref[...]
    waited = False
    while work:
        group, total = [], 0
        while work and total + work[0][4] <= 256:
            group.append(work.pop(0))
            total += group[-1][4]
        hot = []
        for _, _, (slot, _), start, rows in group:
            base = jnp.where(slot >= 0, slot * BLK + start, -BLK)
            line = lax.broadcasted_iota(jnp.int32, (rows, toks), 0)
            hot.append(mm == line + base)
        hot = jnp.concatenate(hot, axis=0).astype(jnp.float32)
        scale = 1.0 / jnp.maximum(jnp.sum(hot, axis=1, keepdims=True), 1.0)
        if not waited:
            copies[2].wait()
            waited = True
        sums = jnp.dot(hot.astype(jnp.bfloat16), tok_ref[...], preferred_element_type=jnp.float32)
        merged = (sums * scale).astype(jnp.bfloat16)
        row = 0
        for out, at, _, _, rows in group:
            for h in range(pieces):
                outs[out][at + h * rows : at + (h + 1) * rows, :] = merged[
                    row : row + rows, h * LANES : (h + 1) * LANES
                ]
            row += rows


def pad(m):
    return -(-m // TAG) * TAG


def is_slot(tag, s):
    return tag[0:1, :].astype(jnp.float32) == float(s)


def masks_of(tags, rows):
    return [[jnp.broadcast_to(is_slot(tag, s), (rows, LANES)) for s in range(OWN)] for tag in tags]


def gather_kernel(m, rows, tagged, *refs):
    blocks = refs[:m]
    if tagged:
        (out_ref,) = refs[m:]
        size = out_ref.shape[0] - pad(m)
        for k in range(m):
            out_ref[size + k : size + k + 1, :] = blocks[k][size // OWN : size // OWN + 1, :]
        tags = [blocks[k][size // OWN : size // OWN + TAG, :] for k in range(m)]
    else:
        known_ref, out_ref = refs[m:]
        size = out_ref.shape[0]
        first = known_ref.shape[0] - pad(m)
        tags = [known_ref[first + k : first + k + 1, :] for k in range(m)]
    masks = masks_of(tags, rows)
    for h in range(0, size // OWN, rows):
        pick = [jnp.zeros((rows, LANES), jnp.bfloat16)] * OWN
        for k in range(m):
            block = blocks[k][h : h + rows, :]
            pick = [jnp.where(masks[k][s], block, pick[s]) for s in range(OWN)]
        for s in range(OWN):
            out_ref[s * (size // OWN) + h : s * (size // OWN) + h + rows, :] = pick[s]


def project_kernel(m, rows, tagged, skip, wq_ref, wk_ref, wv_ref, cross_ref, *refs):
    blocks, refs = refs[:m], refs[m:]
    if tagged:
        q_ref, kv_ref, tag_ref, x_ref = refs
    else:
        tag_ref, q_ref, kv_ref, x_ref = refs
    pieces = x_ref.shape[1] // LANES
    size = pieces * rows
    if tagged:
        for k in range(m):
            tag_ref[k] = blocks[k][skip + size : skip + size + TAG, :]
            tag_ref[m + k] = jnp.broadcast_to(
                cross_ref[OWN * size + k : OWN * size + k + 1, :], (TAG, LANES)
            )
    masks = masks_of([tag_ref[k] for k in range(m)], rows)
    for h in range(pieces):
        pick = [jnp.zeros((rows, LANES), jnp.bfloat16)] * OWN
        for k in range(m):
            block = blocks[k][skip + h * rows : skip + (h + 1) * rows, :]
            pick = [jnp.where(masks[k][s], block, pick[s]) for s in range(OWN)]
        for s in range(OWN):
            other = cross_ref[s * size + h * rows : s * size + (h + 1) * rows, :]
            x_ref[s * rows : (s + 1) * rows, h * LANES : (h + 1) * LANES] = pick[s] + other
    x = x_ref[...]
    width = wk_ref.shape[1]

    def mul(w):
        return jnp.dot(x, w[...], preferred_element_type=jnp.float32).astype(jnp.bfloat16)

    kv_ref[:, :width] = mul(wk_ref)
    kv_ref[:, width:] = mul(wv_ref)
    q_ref[...] = mul(wq_ref)


def attend_kernel(n, n_col, near_ref, tag_ref, *refs):
    my_col = lax.axis_index("col")
    chunks = PARTS
    near = near_ref.shape[1]
    refs = list(refs)
    qs, refs = refs[: len(chunks)], refs[len(chunks) :]
    kvs, refs = refs[: len(chunks) * n_col], refs[len(chunks) * n_col :]
    outs, (kv_ref, head_ref) = refs[:n], refs[n:]
    width = qs[0].shape[1]
    for s in range(OWN):
        place = jnp.int32(0)
        for k in range(n_col):
            col = partner(my_col, k, n_col, True)
            for t in range(OWN):
                cand = col * OWN + t
                hit = near_ref[s, 0] == cand
                for j in range(1, near):
                    hit = hit | (near_ref[s, j] == cand)

                @pl.when(hit)
                def _(place=place):
                    for c, (start, rows) in enumerate(chunks):
                        at = pl.multiple_of(place * BLK + start, 8)
                        kv_ref[s, pl.ds(at, rows), :] = kvs[c * n_col + k][
                            t * rows : (t + 1) * rows, :
                        ]

                place = place + jnp.where(hit, 1, 0)
    scale = 1.0 / math.sqrt(HD)
    low = lax.broadcasted_iota(jnp.int32, (BLK, LANES), 1) < HD
    zero = jnp.zeros((BLK, LANES), jnp.bfloat16)
    for s in range(OWN):
        for h in range(0, width, LANES):
            q = jnp.concatenate(
                [
                    qs[c][s * rows : (s + 1) * rows, h : h + LANES]
                    for c, (_, rows) in enumerate(chunks)
                ],
                axis=0,
            )
            q = jnp.concatenate([jnp.where(low, q, zero), jnp.where(low, zero, q)], axis=0)
            score = lax.dot_general(
                q,
                kv_ref[s, :, h : h + LANES],
                (((1,), (1,)), ((), ())),
                preferred_element_type=jnp.float32,
            )
            score = score * scale
            p = jnp.exp(score - jnp.max(score, axis=1, keepdims=True))
            total = jnp.sum(p, axis=1, keepdims=True)
            o = jnp.dot(
                p.astype(jnp.bfloat16),
                kv_ref[s, :, width + h : width + h + LANES],
                preferred_element_type=jnp.float32,
            )
            o = (o * (1.0 / total)).astype(jnp.bfloat16)
            head_ref[s, :, h : h + LANES] = jnp.where(low, o[:BLK], o[BLK:])
    for k in range(n):
        masks = [
            jnp.broadcast_to(is_slot(tag_ref[k], s), (BLK, LANES)) for s in range(OWN)
        ]
        for h in range(0, width, LANES):
            pick = zero
            for s in range(OWN):
                pick = jnp.where(masks[s], head_ref[s, :, h : h + LANES], pick)
            outs[k][:, h : h + LANES] = pick


def spread_kernel(n, slots, map_ref, owner_ref, out_ref):
    me = lax.axis_index("row")
    mm = map_ref[...]
    block = mm // BLK
    target = mm % BLK
    for k in range(n):
        slot, _ = slot_of(owner_ref, peer(me, k, n), slots)
        target = target + jnp.where((block == slot) & (slot >= 0), k * BLK, 0)
    toks = mm.shape[1]
    for k0 in range(0, n * BLK, LANES):
        ids = lax.broadcasted_iota(jnp.int32, (LANES, toks), 0) + k0
        hot = (ids == target).astype(jnp.float32)
        out_ref[:, k0 : k0 + LANES] = jnp.transpose(hot).astype(jnp.bfloat16)


def return_kernel(n, spread_ref, *refs):
    blocks, out_ref, all_ref = refs[:n], refs[n], refs[n + 1]
    for k in range(n):
        all_ref[k * BLK : (k + 1) * BLK, :] = blocks[k][...]
    out_ref[...] = jnp.dot(
        spread_ref[...], all_ref[...], preferred_element_type=jnp.float32
    ).astype(out_ref.dtype)


def on_device(tokens, merge_map, block_owner, neighbours, w_query, w_key, w_value):
    n = lax.axis_size("row")
    n_col = lax.axis_size("col")
    toks, width = tokens.shape
    heads = w_query.shape[1]
    slots = block_owner.shape[1]
    near = neighbours.shape[1]
    bf16 = jnp.bfloat16

    def shape(*s, dtype=bf16):
        return jax.ShapeDtypeStruct(s, dtype)

    mm = pltpu.with_memory_space_constraint(merge_map.reshape(1, toks), pltpu.HBM)
    tokens = pltpu.with_memory_space_constraint(tokens, pltpu.HBM)
    block_owner = pltpu.with_memory_space_constraint(block_owner, pltpu.HBM)
    neighbours = pltpu.with_memory_space_constraint(neighbours, pltpu.HBM)
    m = n // 2
    pieces = width // LANES

    def merge(*which):
        messages = tuple(MESSAGES[i] for i in which)
        shapes = []
        for message in messages:
            size = sum(part[2] for part in message) * pieces
            size += TAG * any(part[1] == 0 for part in message)
            shapes += [shape(size, LANES)] * m
        outs = pl.pallas_call(
            functools.partial(merge_kernel, n, slots, messages),
            out_shape=shapes,
            in_specs=[HBM] * 3,
            out_specs=[VMEM] * len(shapes),
            scratch_shapes=[
                pltpu.VMEM((toks, width), bf16),
                pltpu.VMEM((1, toks), jnp.int32),
                pltpu.SMEM(block_owner.shape, jnp.int32),
                pltpu.SemaphoreType.DMA((3,)),
            ],
            compiler_params=PARAMS,
            cost_estimate=cost(2),
            name="merge",
        )(tokens, mm, block_owner)
        return [outs[i * m : (i + 1) * m] for i in range(len(which))]

    def gather(c, blocks, *known):
        rows = PARTS[c][1]
        out = pl.pallas_call(
            functools.partial(gather_kernel, m, rows, not known),
            out_shape=shape(OWN * rows * pieces + (0 if known else pad(m)), LANES),
            in_specs=[VMEM] * (m + len(known)),
            out_specs=VMEM,
            compiler_params=PARAMS,
            cost_estimate=cost(0.5),
            name="gather",
        )(*blocks, *known)
        return out, lax.ppermute(out, "row", [(i, across(i, n)) for i in range(n)])

    def project(c, skip, cross, blocks, *tags):
        rows = PARTS[c][1]
        out = pl.pallas_call(
            functools.partial(project_kernel, m, rows, not tags, skip),
            out_shape=[shape(OWN * rows, heads), shape(OWN * rows, 2 * heads)]
            + [shape(n, TAG, LANES)] * (not tags),
            in_specs=[VMEM] * (4 + m + len(tags)),
            out_specs=[VMEM] * (2 + (not tags)),
            scratch_shapes=[pltpu.VMEM((OWN * rows, width), bf16)],
            compiler_params=PARAMS,
            cost_estimate=cost(1),
            name="project",
        )(w_query, w_key, w_value, cross, *blocks, *tags)
        return out, rounds([out[1]] * n_col, "col", n_col, partner)

    (far0,) = merge(0)
    far0 = rounds(far0, "row", n, inner)
    far1, home1 = merge(1, 2)
    far1 = rounds(far1, "row", n, inner)
    known, cross0 = gather(0, far0)
    home1 = rounds(home1, "row", n, inner)
    _, cross1 = gather(1, far1, known)
    (q0, _, tags), kv0 = project(0, SECOND[1] * pieces, cross0, far1)
    (q1, _), kv1 = project(1, 0, cross1, home1, tags)
    qs, kvs = [q0, q1], kv0 + kv1
    spread = pl.pallas_call(
        functools.partial(spread_kernel, n, slots),
        out_shape=shape(toks, n * BLK),
        in_specs=[VMEM, SMEM],
        out_specs=VMEM,
        compiler_params=PARAMS,
        cost_estimate=cost(2),
        name="spread",
    )(mm, block_owner)
    replies = pl.pallas_call(
        functools.partial(attend_kernel, n, n_col),
        out_shape=[shape(BLK, heads)] * n,
        in_specs=[SMEM] + [VMEM] * (1 + len(qs) + len(kvs)),
        out_specs=[VMEM] * n,
        scratch_shapes=[
            pltpu.VMEM((OWN, near * BLK, 2 * heads), bf16),
            pltpu.VMEM((OWN, BLK, heads), bf16),
        ],
        compiler_params=PARAMS,
        cost_estimate=cost(3),
        name="attend",
    )(neighbours, tags, *qs, *kvs)
    returned = rounds(replies, "row", n, functools.partial(peer, back=True))
    return pl.pallas_call(
        functools.partial(return_kernel, n),
        out_shape=shape(toks, heads),
        in_specs=[VMEM] * (1 + n),
        out_specs=VMEM,
        scratch_shapes=[pltpu.VMEM((n * BLK, heads), bf16)],
        compiler_params=PARAMS,
        cost_estimate=cost(2),
        name="give_back",
    )(spread, *returned)


def solution(mesh):
    in_specs = (
        P(("row", "col"), None),
        P(("row", "col")),
        P(("row", "col"), None),
        P(("row", "col"), None),
        P(),
        P(),
        P(),
    )
    out_specs = P(("row", "col"), None)

    return jax.shard_map(
        on_device, mesh=mesh, in_specs=in_specs, out_specs=out_specs, check_vma=False
    )
```

```python
import functools
import math

import jax
import jax.numpy as jnp
from jax import lax
from jax.experimental import pallas as pl
from jax.experimental.pallas import tpu as pltpu
from jax.sharding import PartitionSpec as P


HD = 64
BLK = 64
OWN = 2
LANES = 128
TAG = 8


VMEM = pl.BlockSpec(memory_space=pltpu.VMEM)
SMEM = pl.BlockSpec(memory_space=pltpu.SMEM)
HBM = pl.BlockSpec(memory_space=pltpu.HBM)
PARAMS = pltpu.CompilerParams(vmem_limit_bytes=16 << 20)


def partner(i, k, n, back=False):
    if n & (n - 1) == 0:
        return i ^ k
    return (i - k + n) % n if back else (i + k) % n


def inner(i, k, n, back=False):
    m = n // 2
    side = (i >= m) * m
    return side + partner(i - side, k, m, back)


def across(i, n):
    m = n // 2
    return i + m - (i >= m) * n


def peer(i, k, n, back=False):
    m = n // 2
    return inner(i, k, n, back) if k < m else across(inner(i, k - m, n, back), n)


def order(n):
    return sorted(range(1, n), key=lambda k: (-(k.bit_length() - 1 if k > 1 else 0), k))


def rounds(x, axis, n, to):
    out = list(x)
    for k in order(len(x)):
        out[k] = lax.ppermute(x[k], axis, [(i, to(i, k, n)) for i in range(n)])
    return out


def cost(us):
    return pl.CostEstimate(
        flops=int(us * 8e8), bytes_accessed=int(us * 2e6), transcendentals=0
    )


FIRST = (0, BLK // 2)
SECOND = (BLK // 2, BLK - BLK // 2)
PARTS = (FIRST, SECOND)
MESSAGES = (
    ((True, *FIRST),),
    ((True, *SECOND),),
    ((False, *FIRST),),
    ((False, *SECOND),),
)


def slot_of(owner_ref, row, slots):
    slot = jnp.int32(-1)
    code = jnp.int32(-1)
    for b in range(slots):
        o = owner_ref[0, b]
        hit = (o >= 0) & (o // OWN == row)
        slot = jnp.where(hit, b, slot)
        code = jnp.where(hit, o % OWN, code)
    return slot, code


def merge_kernel(n, slots, messages, tok_hbm, map_hbm, owner_hbm, *refs):
    m = n // 2
    outs = refs[: m * len(messages)]
    tok_ref, map_ref, owner_ref, sems = refs[m * len(messages) :]
    copies = [
        pltpu.make_async_copy(src, dst, sems.at[i])
        for i, (src, dst) in enumerate(
            [(owner_hbm, owner_ref), (map_hbm, map_ref), (tok_hbm, tok_ref)]
        )
    ]
    for copy in copies:
        copy.start()
    me = lax.axis_index("row")
    toks, width = tok_ref.shape
    pieces = width // LANES
    copies[0].wait()
    dest = {}
    for far in sorted({part[0] for message in messages for part in message}):
        for k in range(m):
            to = inner(me, k, n)
            dest[far, k] = slot_of(owner_ref, across(to, n) if far else to, slots)
    work = []
    for i, message in enumerate(messages):
        at = 0
        for far, start, rows in message:
            work += [(i * m + k, at, dest[far, k], start, rows) for k in range(m)]
            at += rows * pieces
            if start == 0:
                end = sum(part[2] for part in message) * pieces
                for k in range(m):
                    outs[i * m + k][end:, :] = jnp.full(
                        (TAG, LANES), dest[far, k][1], jnp.int32
                    ).astype(jnp.bfloat16)
    copies[1].wait()
    mm = map_ref[...]
    waited = False
    while work:
        group, total = [], 0
        while work and total + work[0][4] <= 256:
            group.append(work.pop(0))
            total += group[-1][4]
        hot = []
        for _, _, (slot, _), start, rows in group:
            base = jnp.where(slot >= 0, slot * BLK + start, -BLK)
            line = lax.broadcasted_iota(jnp.int32, (rows, toks), 0)
            hot.append(mm == line + base)
        hot = jnp.concatenate(hot, axis=0).astype(jnp.float32)
        scale = 1.0 / jnp.maximum(jnp.sum(hot, axis=1, keepdims=True), 1.0)
        if not waited:
            copies[2].wait()
            waited = True
        sums = jnp.dot(hot.astype(jnp.bfloat16), tok_ref[...], preferred_element_type=jnp.float32)
        merged = (sums * scale).astype(jnp.bfloat16)
        row = 0
        for out, at, _, _, rows in group:
            for h in range(pieces):
                outs[out][at + h * rows : at + (h + 1) * rows, :] = merged[
                    row : row + rows, h * LANES : (h + 1) * LANES
                ]
            row += rows


def pad(m):
    return -(-m // TAG) * TAG


def is_slot(tag, s):
    return tag[0:1, :].astype(jnp.float32) == float(s)


def masks_of(tags, rows):
    return [[jnp.broadcast_to(is_slot(tag, s), (rows, LANES)) for s in range(OWN)] for tag in tags]


def gather_kernel(m, rows, tagged, *refs):
    blocks = refs[:m]
    if tagged:
        (out_ref,) = refs[m:]
        size = out_ref.shape[0] - pad(m)
        for k in range(m):
            out_ref[size + k : size + k + 1, :] = blocks[k][size // OWN : size // OWN + 1, :]
        tags = [blocks[k][size // OWN : size // OWN + TAG, :] for k in range(m)]
    else:
        known_ref, out_ref = refs[m:]
        size = out_ref.shape[0]
        first = known_ref.shape[0] - pad(m)
        tags = [known_ref[first + k : first + k + 1, :] for k in range(m)]
    masks = masks_of(tags, rows)
    for h in range(0, size // OWN, rows):
        pick = [jnp.zeros((rows, LANES), jnp.bfloat16)] * OWN
        for k in range(m):
            block = blocks[k][h : h + rows, :]
            pick = [jnp.where(masks[k][s], block, pick[s]) for s in range(OWN)]
        for s in range(OWN):
            out_ref[s * (size // OWN) + h : s * (size // OWN) + h + rows, :] = pick[s]


def project_kernel(m, rows, tagged, wq_ref, wk_ref, wv_ref, cross_ref, *refs):
    blocks, refs = refs[:m], refs[m:]
    if tagged:
        q_ref, kv_ref, tag_ref, x_ref = refs
    else:
        tag_ref, q_ref, kv_ref, x_ref = refs
    pieces = x_ref.shape[1] // LANES
    size = pieces * rows
    if tagged:
        for k in range(m):
            tag_ref[k] = blocks[k][size : size + TAG, :]
            tag_ref[m + k] = jnp.broadcast_to(
                cross_ref[OWN * size + k : OWN * size + k + 1, :], (TAG, LANES)
            )
    masks = masks_of([tag_ref[k] for k in range(m)], rows)
    for h in range(pieces):
        pick = [jnp.zeros((rows, LANES), jnp.bfloat16)] * OWN
        for k in range(m):
            block = blocks[k][h * rows : (h + 1) * rows, :]
            pick = [jnp.where(masks[k][s], block, pick[s]) for s in range(OWN)]
        for s in range(OWN):
            other = cross_ref[s * size + h * rows : s * size + (h + 1) * rows, :]
            x_ref[s * rows : (s + 1) * rows, h * LANES : (h + 1) * LANES] = pick[s] + other
    x = x_ref[...]
    width = wk_ref.shape[1]

    def mul(w):
        return jnp.dot(x, w[...], preferred_element_type=jnp.float32).astype(jnp.bfloat16)

    kv_ref[:, :width] = mul(wk_ref)
    kv_ref[:, width:] = mul(wv_ref)
    q_ref[...] = mul(wq_ref)


def attend_kernel(n, n_col, near_ref, tag_ref, *refs):
    my_col = lax.axis_index("col")
    chunks = PARTS
    near = near_ref.shape[1]
    refs = list(refs)
    qs, refs = refs[: len(chunks)], refs[len(chunks) :]
    kvs, refs = refs[: len(chunks) * n_col], refs[len(chunks) * n_col :]
    outs, (kv_ref, head_ref) = refs[:n], refs[n:]
    width = qs[0].shape[1]
    for s in range(OWN):
        place = jnp.int32(0)
        for k in range(n_col):
            col = partner(my_col, k, n_col, True)
            for t in range(OWN):
                cand = col * OWN + t
                hit = near_ref[s, 0] == cand
                for j in range(1, near):
                    hit = hit | (near_ref[s, j] == cand)

                @pl.when(hit)
                def _(place=place):
                    for c, (start, rows) in enumerate(chunks):
                        at = pl.multiple_of(place * BLK + start, 8)
                        kv_ref[s, pl.ds(at, rows), :] = kvs[c * n_col + k][
                            t * rows : (t + 1) * rows, :
                        ]

                place = place + jnp.where(hit, 1, 0)
    scale = 1.0 / math.sqrt(HD)
    low = lax.broadcasted_iota(jnp.int32, (BLK, LANES), 1) < HD
    zero = jnp.zeros((BLK, LANES), jnp.bfloat16)
    for s in range(OWN):
        for h in range(0, width, LANES):
            q = jnp.concatenate(
                [
                    qs[c][s * rows : (s + 1) * rows, h : h + LANES]
                    for c, (_, rows) in enumerate(chunks)
                ],
                axis=0,
            )
            q = jnp.concatenate([jnp.where(low, q, zero), jnp.where(low, zero, q)], axis=0)
            score = lax.dot_general(
                q,
                kv_ref[s, :, h : h + LANES],
                (((1,), (1,)), ((), ())),
                preferred_element_type=jnp.float32,
            )
            score = score * scale
            p = jnp.exp(score - jnp.max(score, axis=1, keepdims=True))
            total = jnp.sum(p, axis=1, keepdims=True)
            o = jnp.dot(
                p.astype(jnp.bfloat16),
                kv_ref[s, :, width + h : width + h + LANES],
                preferred_element_type=jnp.float32,
            )
            o = (o * (1.0 / total)).astype(jnp.bfloat16)
            head_ref[s, :, h : h + LANES] = jnp.where(low, o[:BLK], o[BLK:])
    for k in range(n):
        masks = [
            jnp.broadcast_to(is_slot(tag_ref[k], s), (BLK, LANES)) for s in range(OWN)
        ]
        for h in range(0, width, LANES):
            pick = zero
            for s in range(OWN):
                pick = jnp.where(masks[s], head_ref[s, :, h : h + LANES], pick)
            outs[k][:, h : h + LANES] = pick


def spread_kernel(n, slots, map_ref, owner_ref, out_ref):
    me = lax.axis_index("row")
    mm = map_ref[...]
    block = mm // BLK
    target = mm % BLK
    for k in range(n):
        slot, _ = slot_of(owner_ref, peer(me, k, n), slots)
        target = target + jnp.where((block == slot) & (slot >= 0), k * BLK, 0)
    toks = mm.shape[1]
    for k0 in range(0, n * BLK, LANES):
        ids = lax.broadcasted_iota(jnp.int32, (LANES, toks), 0) + k0
        hot = (ids == target).astype(jnp.float32)
        out_ref[:, k0 : k0 + LANES] = jnp.transpose(hot).astype(jnp.bfloat16)


def return_kernel(n, spread_ref, *refs):
    blocks, out_ref, all_ref = refs[:n], refs[n], refs[n + 1]
    for k in range(n):
        all_ref[k * BLK : (k + 1) * BLK, :] = blocks[k][...]
    out_ref[...] = jnp.dot(
        spread_ref[...], all_ref[...], preferred_element_type=jnp.float32
    ).astype(out_ref.dtype)


def on_device(tokens, merge_map, block_owner, neighbours, w_query, w_key, w_value):
    n = lax.axis_size("row")
    n_col = lax.axis_size("col")
    toks, width = tokens.shape
    heads = w_query.shape[1]
    slots = block_owner.shape[1]
    near = neighbours.shape[1]
    bf16 = jnp.bfloat16

    def shape(*s, dtype=bf16):
        return jax.ShapeDtypeStruct(s, dtype)

    mm = pltpu.with_memory_space_constraint(merge_map.reshape(1, toks), pltpu.HBM)
    tokens = pltpu.with_memory_space_constraint(tokens, pltpu.HBM)
    block_owner = pltpu.with_memory_space_constraint(block_owner, pltpu.HBM)
    neighbours = pltpu.with_memory_space_constraint(neighbours, pltpu.HBM)
    m = n // 2
    pieces = width // LANES

    def merge(*which):
        messages = tuple(MESSAGES[i] for i in which)
        shapes = []
        for message in messages:
            size = sum(part[2] for part in message) * pieces
            size += TAG * any(part[1] == 0 for part in message)
            shapes += [shape(size, LANES)] * m
        outs = pl.pallas_call(
            functools.partial(merge_kernel, n, slots, messages),
            out_shape=shapes,
            in_specs=[HBM] * 3,
            out_specs=[VMEM] * len(shapes),
            scratch_shapes=[
                pltpu.VMEM((toks, width), bf16),
                pltpu.VMEM((1, toks), jnp.int32),
                pltpu.SMEM(block_owner.shape, jnp.int32),
                pltpu.SemaphoreType.DMA((3,)),
            ],
            compiler_params=PARAMS,
            cost_estimate=cost(2),
            name="merge",
        )(tokens, mm, block_owner)
        return [outs[i * m : (i + 1) * m] for i in range(len(which))]

    def gather(c, blocks, *known):
        rows = PARTS[c][1]
        out = pl.pallas_call(
            functools.partial(gather_kernel, m, rows, not known),
            out_shape=shape(OWN * rows * pieces + (0 if known else pad(m)), LANES),
            in_specs=[VMEM] * (m + len(known)),
            out_specs=VMEM,
            compiler_params=PARAMS,
            cost_estimate=cost(0.5),
            name="gather",
        )(*blocks, *known)
        return out, lax.ppermute(out, "row", [(i, across(i, n)) for i in range(n)])

    def project(c, cross, blocks, *tags):
        rows = PARTS[c][1]
        out = pl.pallas_call(
            functools.partial(project_kernel, m, rows, not tags),
            out_shape=[shape(OWN * rows, heads), shape(OWN * rows, 2 * heads)]
            + [shape(n, TAG, LANES)] * (not tags),
            in_specs=[VMEM] * (4 + m + len(tags)),
            out_specs=[VMEM] * (2 + (not tags)),
            scratch_shapes=[pltpu.VMEM((OWN * rows, width), bf16)],
            compiler_params=PARAMS,
            cost_estimate=cost(1),
            name="project",
        )(w_query, w_key, w_value, cross, *blocks, *tags)
        return out, rounds([out[1]] * n_col, "col", n_col, partner)

    (far0,) = merge(0)
    far0 = rounds(far0, "row", n, inner)
    far1, own0, own1 = merge(1, 2, 3)
    far1 = rounds(far1, "row", n, inner)
    known, cross0 = gather(0, far0)
    own0 = rounds(own0, "row", n, inner)
    own1 = rounds(own1, "row", n, inner)
    _, cross1 = gather(1, far1, known)
    (q0, _, tags), kv0 = project(0, cross0, own0)
    (q1, _), kv1 = project(1, cross1, own1, tags)
    qs, kvs = [q0, q1], kv0 + kv1
    spread = pl.pallas_call(
        functools.partial(spread_kernel, n, slots),
        out_shape=shape(toks, n * BLK),
        in_specs=[VMEM, SMEM],
        out_specs=VMEM,
        compiler_params=PARAMS,
        cost_estimate=cost(2),
        name="spread",
    )(mm, block_owner)
    replies = pl.pallas_call(
        functools.partial(attend_kernel, n, n_col),
        out_shape=[shape(BLK, heads)] * n,
        in_specs=[SMEM] + [VMEM] * (1 + len(qs) + len(kvs)),
        out_specs=[VMEM] * n,
        scratch_shapes=[
            pltpu.VMEM((OWN, near * BLK, 2 * heads), bf16),
            pltpu.VMEM((OWN, BLK, heads), bf16),
        ],
        compiler_params=PARAMS,
        cost_estimate=cost(3),
        name="attend",
    )(neighbours, tags, *qs, *kvs)
    returned = rounds(replies, "row", n, functools.partial(peer, back=True))
    return pl.pallas_call(
        functools.partial(return_kernel, n),
        out_shape=shape(toks, heads),
        in_specs=[VMEM] * (1 + n),
        out_specs=VMEM,
        scratch_shapes=[pltpu.VMEM((n * BLK, heads), bf16)],
        compiler_params=PARAMS,
        cost_estimate=cost(2),
        name="give_back",
    )(spread, *returned)


def solution(mesh):
    in_specs = (
        P(("row", "col"), None),
        P(("row", "col")),
        P(("row", "col"), None),
        P(("row", "col"), None),
        P(),
        P(),
        P(),
    )
    out_specs = P(("row", "col"), None)

    return jax.shard_map(
        on_device, mesh=mesh, in_specs=in_specs, out_specs=out_specs, check_vma=False
    )
```

```python
import functools
import math

import jax
import jax.numpy as jnp
from jax import lax
from jax.experimental import pallas as pl
from jax.experimental.pallas import tpu as pltpu
from jax.sharding import PartitionSpec as P


HD = 64
BLK = 64
OWN = 2
LANES = 128
TAG = 8
STRIP = 8
RETURN_STEPS = 4


VMEM = pl.BlockSpec(memory_space=pltpu.VMEM)
SMEM = pl.BlockSpec(memory_space=pltpu.SMEM)
HBM = pl.BlockSpec(memory_space=pltpu.HBM)
PARAMS = pltpu.CompilerParams(vmem_limit_bytes=16 << 20)


def partner(i, k, n, back=False):
    if n & (n - 1) == 0:
        return i ^ k
    return (i - k + n) % n if back else (i + k) % n


def inner(i, k, n, back=False):
    m = n // 2
    side = (i >= m) * m
    return side + partner(i - side, k, m, back)


def across(i, n):
    m = n // 2
    return i + m - (i >= m) * n


def peer(i, k, n, back=False):
    m = n // 2
    return inner(i, k, n, back) if k < m else across(inner(i, k - m, n, back), n)


def order(n):
    return sorted(range(1, n), key=lambda k: (-(k.bit_length() - 1 if k > 1 else 0), k))


def rounds(x, axis, n, to):
    out = list(x)
    for k in order(len(x)):
        out[k] = lax.ppermute(x[k], axis, [(i, to(i, k, n)) for i in range(n)])
    return out


def cost(us):
    return pl.CostEstimate(
        flops=int(us * 8e8), bytes_accessed=int(us * 2e6), transcendentals=0
    )


FIRST = (0, BLK // 2)
SECOND = (BLK // 2, BLK - BLK // 2)
PARTS = (FIRST, SECOND)
HOME = ((0, BLK),)
MESSAGES = (
    ((True, *FIRST),),
    ((True, *SECOND),),
    ((False, *FIRST),),
    ((False, *SECOND),),
)


def slot_of(owner_ref, row, slots):
    slot = jnp.int32(-1)
    code = jnp.int32(-1)
    for b in range(slots):
        o = owner_ref[0, b]
        hit = (o >= 0) & (o // OWN == row)
        slot = jnp.where(hit, b, slot)
        code = jnp.where(hit, o % OWN, code)
    return slot, code


def rows_of(message):
    return sum(part[2] for part in message)


def merge_rows(hot, tok_ref, spots, pieces, ready):
    hot = hot.astype(jnp.float32)
    scale = 1.0 / jnp.maximum(jnp.sum(hot, axis=1, keepdims=True), 1.0)
    hot = hot.astype(jnp.bfloat16)
    for c in range(0, pieces, STRIP):
        ready(c // STRIP)
        columns = tok_ref[:, c * LANES : (c + STRIP) * LANES]
        sums = jnp.dot(hot, columns, preferred_element_type=jnp.float32)
        merged = (sums * scale).astype(jnp.bfloat16)
        row = 0
        for ref, rows in spots:
            for h in range(STRIP):
                at = (c + h) * rows
                ref[at : at + rows, :] = merged[row : row + rows, h * LANES : (h + 1) * LANES]
            row += rows


def first_merge_kernel(n, slots, tok_hbm, map_hbm, owner_hbm, *refs):
    m = n // 2
    outs = refs[:m]
    tok_ref, map_ref, ids_ref, code_ref, owner_ref, sems = refs[m:]
    _, width = tok_ref.shape
    pieces = width // LANES
    strips = [
        pltpu.make_async_copy(
            tok_hbm.at[:, c * LANES : (c + STRIP) * LANES],
            tok_ref.at[:, c * LANES : (c + STRIP) * LANES],
            sems.at[2 + c // STRIP],
        )
        for c in range(0, pieces, STRIP)
    ]
    get_owner = pltpu.make_async_copy(owner_hbm, owner_ref, sems.at[0])
    get_map = pltpu.make_async_copy(map_hbm, map_ref, sems.at[1])
    for copy in (get_owner, get_map, *strips):
        copy.start()
    me = lax.axis_index("row")
    get_owner.wait()
    to = [inner(me, k, n) for k in range(m)]
    near = [slot_of(owner_ref, to[k], slots) for k in range(m)]
    far = [slot_of(owner_ref, across(to[k], n), slots) for k in range(m)]

    def ids(slot, start, rows):
        base = jnp.where(slot >= 0, slot * BLK + start, -BLK)
        return lax.broadcasted_iota(jnp.int32, (rows, LANES), 0) + base

    (_, start, rows), pieces_rows = MESSAGES[0][0], pieces * MESSAGES[0][0][2]
    for k in range(m):
        outs[k][pieces_rows:, :] = jnp.full((TAG, LANES), far[k][1], jnp.int32).astype(
            jnp.bfloat16
        )
        code_ref[k * TAG : (k + 1) * TAG, :] = jnp.full(
            (TAG, LANES), near[k][1], jnp.int32
        ).astype(jnp.bfloat16)
    mine = jnp.concatenate([ids(far[k][0], start, rows)[:, :1] for k in range(m)], axis=0)
    get_map.wait()
    merge_rows(
        map_ref[...] == mine,
        tok_ref,
        [(outs[k], rows) for k in range(m)],
        pieces,
        lambda c: strips[c].wait(),
    )
    at = 0
    for message in MESSAGES[1:]:
        ((other, start, rows),) = message
        for k in range(m):
            ids_ref[at : at + rows, :] = ids((far if other else near)[k][0], start, rows)
            at += rows


def later_merge_kernel(m, tok_ref, map_ref, ids_ref, code_ref, *outs):
    pieces = tok_ref.shape[1] // LANES
    at = 0
    for i, message in enumerate(MESSAGES[1:]):
        ((other, start, rows),) = message
        hot = map_ref[...] == ids_ref[at : at + m * rows, :1]
        spots = [(outs[i * m + k], rows) for k in range(m)]
        merge_rows(hot, tok_ref, spots, pieces, lambda c: None)
        if start == 0:
            for k in range(m):
                outs[i * m + k][pieces * rows :, :] = code_ref[k * TAG : (k + 1) * TAG, :]
        at += m * rows


def pad(m):
    return -(-m // TAG) * TAG


def is_slot(tag, s):
    return tag[0:1, :].astype(jnp.float32) == float(s)


def masks_of(tags, rows):
    return [[jnp.broadcast_to(is_slot(tag, s), (rows, LANES)) for s in range(OWN)] for tag in tags]


def gather_kernel(m, rows, tagged, *refs):
    blocks = refs[:m]
    if tagged:
        (out_ref,) = refs[m:]
        size = out_ref.shape[0] - pad(m)
        for k in range(m):
            out_ref[size + k : size + k + 1, :] = blocks[k][size // OWN : size // OWN + 1, :]
        tags = [blocks[k][size // OWN : size // OWN + TAG, :] for k in range(m)]
    else:
        known_ref, out_ref = refs[m:]
        size = out_ref.shape[0]
        first = known_ref.shape[0] - pad(m)
        tags = [known_ref[first + k : first + k + 1, :] for k in range(m)]
    masks = masks_of(tags, rows)
    for h in range(0, size // OWN, rows):
        pick = [jnp.zeros((rows, LANES), jnp.bfloat16)] * OWN
        for k in range(m):
            block = blocks[k][h : h + rows, :]
            pick = [jnp.where(masks[k][s], block, pick[s]) for s in range(OWN)]
        for s in range(OWN):
            out_ref[s * (size // OWN) + h : s * (size // OWN) + h + rows, :] = pick[s]


def project_kernel(m, rows, tagged, wq_ref, wk_ref, wv_ref, cross_ref, *refs):
    blocks, refs = refs[:m], refs[m:]
    if tagged:
        q_ref, kv_ref, tag_ref, x_ref = refs
    else:
        tag_ref, q_ref, kv_ref, x_ref = refs
    pieces = x_ref.shape[1] // LANES
    size = pieces * rows
    if tagged:
        for k in range(m):
            tag_ref[k] = blocks[k][size : size + TAG, :]
    masks = masks_of([tag_ref[k] for k in range(m)], rows)
    for h in range(pieces):
        pick = [jnp.zeros((rows, LANES), jnp.bfloat16)] * OWN
        for k in range(m):
            block = blocks[k][h * rows : (h + 1) * rows, :]
            pick = [jnp.where(masks[k][s], block, pick[s]) for s in range(OWN)]
        for s in range(OWN):
            other = cross_ref[s * size + h * rows : s * size + (h + 1) * rows, :]
            x_ref[s * rows : (s + 1) * rows, h * LANES : (h + 1) * LANES] = pick[s] + other
    x = x_ref[...]
    width = wk_ref.shape[1]

    def mul(w):
        return jnp.dot(x, w[...], preferred_element_type=jnp.float32).astype(jnp.bfloat16)

    kv_ref[:, :width] = mul(wk_ref)
    kv_ref[:, width:] = mul(wv_ref)
    q_ref[...] = mul(wq_ref)


def attend_kernel(m, n_col, tag_ref, bias_ref, *refs):
    refs = list(refs)
    qs, refs = refs[: len(PARTS)], refs[len(PARTS) :]
    kvs, refs = refs[: len(PARTS) * n_col], refs[len(PARTS) * n_col :]
    outs, backs, (head_ref,) = refs[:m], refs[m : m + len(HOME)], refs[m + len(HOME) :]
    width = qs[0].shape[1]
    scale = 1.0 / math.sqrt(HD)
    low = lax.broadcasted_iota(jnp.int32, (BLK, LANES), 1) < HD
    zero = jnp.zeros((BLK, LANES), jnp.bfloat16)
    keys = bias_ref.shape[1]
    bias = jnp.concatenate(
        [jnp.broadcast_to(bias_ref[s : s + 1, :], (2 * BLK, keys)) for s in range(OWN)], axis=0
    )
    for h in range(0, width, LANES):
        rows = []
        for s in range(OWN):
            q = jnp.concatenate(
                [
                    qs[c][s * size : (s + 1) * size, h : h + LANES]
                    for c, (_, size) in enumerate(PARTS)
                ],
                axis=0,
            )
            rows += [jnp.where(low, q, zero), jnp.where(low, zero, q)]
        key = jnp.concatenate([kv[:, h : h + LANES] for kv in kvs], axis=0)
        value = jnp.concatenate([kv[:, width + h : width + h + LANES] for kv in kvs], axis=0)
        score = lax.dot_general(
            jnp.concatenate(rows, axis=0),
            key,
            (((1,), (1,)), ((), ())),
            preferred_element_type=jnp.float32,
        )
        score = score * scale + bias
        p = jnp.exp(score - jnp.max(score, axis=1, keepdims=True))
        total = jnp.sum(p, axis=1, keepdims=True)
        o = jnp.dot(p.astype(jnp.bfloat16), value, preferred_element_type=jnp.float32)
        o = (o * (1.0 / total)).astype(jnp.bfloat16)
        for s in range(OWN):
            at = 2 * s * BLK
            head_ref[s, :, h : h + LANES] = jnp.where(
                low, o[at : at + BLK], o[at + BLK : at + 2 * BLK]
            )
    for back, (start, rows) in zip(backs, HOME):
        for s in range(OWN):
            back[s * rows : (s + 1) * rows, :] = head_ref[s, start : start + rows, :]
    masks = masks_of([tag_ref[k] for k in range(m)], BLK)
    for k in range(m):
        for h in range(0, width, LANES):
            pick = zero
            for s in range(OWN):
                pick = jnp.where(masks[k][s], head_ref[s, :, h : h + LANES], pick)
            outs[k][:, h : h + LANES] = pick


def relay_kernel(m, known_ref, back_ref, *outs):
    rows, width = outs[0].shape
    first = known_ref.shape[0] - pad(m)
    masks = masks_of([known_ref[first + k : first + k + 1, :] for k in range(m)], rows)
    zero = jnp.zeros((rows, LANES), jnp.bfloat16)
    for k in range(m):
        for h in range(0, width, LANES):
            pick = zero
            for s in range(OWN):
                block = back_ref[s * rows : (s + 1) * rows, h : h + LANES]
                pick = jnp.where(masks[k][s], block, pick)
            outs[k][:, h : h + LANES] = pick


def spread_kernel(n, n_col, slots, map_ref, owner_ref, near_ref, out_ref, bias_ref):
    me = lax.axis_index("row")
    my_col = lax.axis_index("col")
    near = near_ref.shape[1]
    at = 0
    for _, rows in PARTS:
        for k in range(n_col):
            for t in range(OWN):
                cand = partner(my_col, k, n_col, True) * OWN + t
                for s in range(OWN):
                    hit = near_ref[s, 0] == cand
                    for j in range(1, near):
                        hit = hit | (near_ref[s, j] == cand)
                    bias_ref[s : s + 1, at : at + rows] = jnp.full(
                        (1, rows), jnp.where(hit, 0.0, -1e30), jnp.float32
                    )
                at += rows
    mm = map_ref[...]
    block = mm // BLK
    target = mm % BLK
    for k in range(n):
        slot, _ = slot_of(owner_ref, peer(me, k, n), slots)
        target = target + jnp.where((block == slot) & (slot >= 0), k * BLK, 0)
    toks = mm.shape[1]
    for k0 in range(0, n * BLK, LANES):
        ids = lax.broadcasted_iota(jnp.int32, (LANES, toks), 0) + k0
        hot = (ids == target).astype(jnp.float32)
        out_ref[:, k0 : k0 + LANES] = jnp.transpose(hot).astype(jnp.bfloat16)


def return_kernel(n, spread_ref, *refs):
    m = n // 2
    blocks, (out_hbm, all_ref, out_ref, sems) = refs[:-4], refs[-4:]
    for k in range(m):
        all_ref[k * BLK : (k + 1) * BLK, :] = blocks[k][...]
        for c, (start, rows) in enumerate(HOME):
            at = (m + k) * BLK + start
            all_ref[at : at + rows, :] = blocks[(1 + c) * m + k][...]
    step = out_ref.shape[0] // RETURN_STEPS
    copies = []
    for i in range(RETURN_STEPS):
        rows = slice(i * step, (i + 1) * step)
        out_ref[rows, :] = jnp.dot(
            spread_ref[rows, :], all_ref[...], preferred_element_type=jnp.float32
        ).astype(out_ref.dtype)
        copies.append(
            pltpu.make_async_copy(out_ref.at[rows, :], out_hbm.at[rows, :], sems.at[i])
        )
        copies[-1].start()
    for copy in copies:
        copy.wait()


def on_device(tokens, merge_map, block_owner, neighbours, w_query, w_key, w_value):
    n = lax.axis_size("row")
    n_col = lax.axis_size("col")
    toks, width = tokens.shape
    heads = w_query.shape[1]
    slots = block_owner.shape[1]
    bf16 = jnp.bfloat16

    def shape(*s, dtype=bf16):
        return jax.ShapeDtypeStruct(s, dtype)

    mm = pltpu.with_memory_space_constraint(merge_map.reshape(1, toks), pltpu.HBM)
    tokens = pltpu.with_memory_space_constraint(tokens, pltpu.HBM)
    block_owner = pltpu.with_memory_space_constraint(block_owner, pltpu.HBM)
    neighbours = pltpu.with_memory_space_constraint(neighbours, pltpu.HBM)
    m = n // 2
    pieces = width // LANES

    def message_shapes(message):
        size = rows_of(message) * pieces + TAG * any(part[1] == 0 for part in message)
        return [shape(size, LANES)] * m

    rest = sum(rows_of(message) for message in MESSAGES[1:]) * m
    *far0, toks_in, map_in, ids, codes = pl.pallas_call(
        functools.partial(first_merge_kernel, n, slots),
        out_shape=message_shapes(MESSAGES[0])
        + [
            shape(toks, width),
            shape(1, toks, dtype=jnp.int32),
            shape(rest, LANES, dtype=jnp.int32),
            shape(m * TAG, LANES),
        ],
        in_specs=[HBM] * 3,
        out_specs=[VMEM] * (m + 4),
        scratch_shapes=[
            pltpu.SMEM(block_owner.shape, jnp.int32),
            pltpu.SemaphoreType.DMA((2 + pieces // STRIP,)),
        ],
        compiler_params=PARAMS,
        cost_estimate=cost(2),
        name="merge",
    )(tokens, mm, block_owner)
    far0 = rounds(far0, "row", n, inner)
    outs = pl.pallas_call(
        functools.partial(later_merge_kernel, m),
        out_shape=[x for message in MESSAGES[1:] for x in message_shapes(message)],
        in_specs=[VMEM] * 4,
        out_specs=[VMEM] * (3 * m),
        compiler_params=PARAMS,
        cost_estimate=cost(2),
        name="merge_rest",
    )(toks_in, map_in, ids, codes)
    far1, own0, own1 = outs[:m], outs[m : 2 * m], outs[2 * m :]

    def gather(c, blocks, *known):
        rows = PARTS[c][1]
        out = pl.pallas_call(
            functools.partial(gather_kernel, m, rows, not known),
            out_shape=shape(OWN * rows * pieces + (0 if known else pad(m)), LANES),
            in_specs=[VMEM] * (m + len(known)),
            out_specs=VMEM,
            compiler_params=PARAMS,
            cost_estimate=cost(0.5),
            name="gather",
        )(*blocks, *known)
        return out, lax.ppermute(out, "row", [(i, across(i, n)) for i in range(n)])

    def project(c, cross, blocks, *tags):
        rows = PARTS[c][1]
        out = pl.pallas_call(
            functools.partial(project_kernel, m, rows, not tags),
            out_shape=[shape(OWN * rows, heads), shape(OWN * rows, 2 * heads)]
            + [shape(m, TAG, LANES)] * (not tags),
            in_specs=[VMEM] * (4 + m + len(tags)),
            out_specs=[VMEM] * (2 + (not tags)),
            scratch_shapes=[pltpu.VMEM((OWN * rows, width), bf16)],
            compiler_params=PARAMS,
            cost_estimate=cost(1),
            name="project",
        )(w_query, w_key, w_value, cross, *blocks, *tags)
        return out, rounds([out[1]] * n_col, "col", n_col, partner)

    far1 = rounds(far1, "row", n, inner)
    known, cross0 = gather(0, far0)
    own0 = rounds(own0, "row", n, inner)
    own1 = rounds(own1, "row", n, inner)
    _, cross1 = gather(1, far1, known)
    (q0, _, tags), kv0 = project(0, cross0, own0)
    (q1, _), kv1 = project(1, cross1, own1, tags)
    qs, kvs = [q0, q1], kv0 + kv1
    spread, bias = pl.pallas_call(
        functools.partial(spread_kernel, n, n_col, slots),
        out_shape=[
            shape(toks, n * BLK),
            shape(TAG, n_col * OWN * BLK, dtype=jnp.float32),
        ],
        in_specs=[VMEM, SMEM, SMEM],
        out_specs=[VMEM, VMEM],
        compiler_params=PARAMS,
        cost_estimate=cost(2),
        name="spread",
    )(map_in, block_owner, neighbours)
    outs = pl.pallas_call(
        functools.partial(attend_kernel, m, n_col),
        out_shape=[shape(BLK, heads)] * m + [shape(OWN * rows, heads) for _, rows in HOME],
        in_specs=[VMEM] * (2 + len(qs) + len(kvs)),
        out_specs=[VMEM] * (m + len(HOME)),
        scratch_shapes=[pltpu.VMEM((OWN, BLK, heads), bf16)],
        compiler_params=PARAMS,
        cost_estimate=cost(3),
        name="attend",
    )(tags, bias, *qs, *kvs)
    backs = [lax.ppermute(back, "row", [(i, across(i, n)) for i in range(n)]) for back in outs[m:]]
    to_sender = functools.partial(inner, back=True)
    returned = rounds(outs[:m], "row", n, to_sender)
    for c, (_, rows) in enumerate(HOME):
        relayed = pl.pallas_call(
            functools.partial(relay_kernel, m),
            out_shape=[shape(rows, heads)] * m,
            in_specs=[VMEM] * 2,
            out_specs=[VMEM] * m,
            compiler_params=PARAMS,
            cost_estimate=cost(0.5),
            name="relay",
        )(known, backs[c])
        returned += rounds(relayed, "row", n, to_sender)
    return pl.pallas_call(
        functools.partial(return_kernel, n),
        out_shape=shape(toks, heads),
        in_specs=[VMEM] * (1 + len(returned)),
        out_specs=HBM,
        scratch_shapes=[
            pltpu.VMEM((n * BLK, heads), bf16),
            pltpu.VMEM((toks, heads), bf16),
            pltpu.SemaphoreType.DMA((RETURN_STEPS,)),
        ],
        compiler_params=PARAMS,
        cost_estimate=cost(2),
        name="give_back",
    )(spread, *returned)


def solution(mesh):
    in_specs = (
        P(("row", "col"), None),
        P(("row", "col")),
        P(("row", "col"), None),
        P(("row", "col"), None),
        P(),
        P(),
        P(),
    )
    out_specs = P(("row", "col"), None)

    return jax.shard_map(
        on_device, mesh=mesh, in_specs=in_specs, out_specs=out_specs, check_vma=False
    )
```

```python
import functools
import math

import jax
import jax.numpy as jnp
from jax import lax
from jax.experimental import pallas as pl
from jax.experimental.pallas import tpu as pltpu
from jax.sharding import PartitionSpec as P


HD = 64
BLK = 64
OWN = 2
LANES = 128
TAG = 8
STRIP = 8
RETURN_STEPS = 4


VMEM = pl.BlockSpec(memory_space=pltpu.VMEM)
SMEM = pl.BlockSpec(memory_space=pltpu.SMEM)
HBM = pl.BlockSpec(memory_space=pltpu.HBM)
PARAMS = pltpu.CompilerParams(vmem_limit_bytes=16 << 20)


def partner(i, k, n, back=False):
    if n & (n - 1) == 0:
        return i ^ k
    return (i - k + n) % n if back else (i + k) % n


def inner(i, k, n, back=False):
    m = n // 2
    side = (i >= m) * m
    return side + partner(i - side, k, m, back)


def across(i, n):
    m = n // 2
    return i + m - (i >= m) * n


def peer(i, k, n, back=False):
    m = n // 2
    return inner(i, k, n, back) if k < m else across(inner(i, k - m, n, back), n)


def order(n):
    return sorted(range(1, n), key=lambda k: (-(k.bit_length() - 1 if k > 1 else 0), k))


def rounds(x, axis, n, to):
    out = list(x)
    for k in order(len(x)):
        out[k] = lax.ppermute(x[k], axis, [(i, to(i, k, n)) for i in range(n)])
    return out


def cost(us):
    return pl.CostEstimate(
        flops=int(us * 8e8), bytes_accessed=int(us * 2e6), transcendentals=0
    )


FIRST = (0, BLK // 2)
SECOND = (BLK // 2, BLK - BLK // 2)
PARTS = (FIRST, SECOND)
MESSAGES = (
    ((True, *FIRST),),
    ((True, *SECOND),),
    ((False, *FIRST),),
    ((False, *SECOND),),
)


def slot_of(owner_ref, row, slots):
    slot = jnp.int32(-1)
    code = jnp.int32(-1)
    for b in range(slots):
        o = owner_ref[0, b]
        hit = (o >= 0) & (o // OWN == row)
        slot = jnp.where(hit, b, slot)
        code = jnp.where(hit, o % OWN, code)
    return slot, code


def rows_of(message):
    return sum(part[2] for part in message)


def merge_rows(hot, tok_ref, spots, pieces, ready):
    hot = hot.astype(jnp.float32)
    scale = 1.0 / jnp.maximum(jnp.sum(hot, axis=1, keepdims=True), 1.0)
    hot = hot.astype(jnp.bfloat16)
    for c in range(0, pieces, STRIP):
        ready(c // STRIP)
        columns = tok_ref[:, c * LANES : (c + STRIP) * LANES]
        sums = jnp.dot(hot, columns, preferred_element_type=jnp.float32)
        merged = (sums * scale).astype(jnp.bfloat16)
        row = 0
        for ref, rows in spots:
            for h in range(STRIP):
                at = (c + h) * rows
                ref[at : at + rows, :] = merged[row : row + rows, h * LANES : (h + 1) * LANES]
            row += rows


def first_merge_kernel(n, slots, tok_hbm, map_hbm, owner_hbm, *refs):
    m = n // 2
    outs = refs[:m]
    tok_ref, map_ref, ids_ref, code_ref, owner_ref, sems = refs[m:]
    _, width = tok_ref.shape
    pieces = width // LANES
    strips = [
        pltpu.make_async_copy(
            tok_hbm.at[:, c * LANES : (c + STRIP) * LANES],
            tok_ref.at[:, c * LANES : (c + STRIP) * LANES],
            sems.at[2 + c // STRIP],
        )
        for c in range(0, pieces, STRIP)
    ]
    get_owner = pltpu.make_async_copy(owner_hbm, owner_ref, sems.at[0])
    get_map = pltpu.make_async_copy(map_hbm, map_ref, sems.at[1])
    for copy in (get_owner, get_map, *strips):
        copy.start()
    me = lax.axis_index("row")
    get_owner.wait()
    to = [inner(me, k, n) for k in range(m)]
    near = [slot_of(owner_ref, to[k], slots) for k in range(m)]
    far = [slot_of(owner_ref, across(to[k], n), slots) for k in range(m)]

    def ids(slot, start, rows):
        base = jnp.where(slot >= 0, slot * BLK + start, -BLK)
        return lax.broadcasted_iota(jnp.int32, (rows, LANES), 0) + base

    (_, start, rows), pieces_rows = MESSAGES[0][0], pieces * MESSAGES[0][0][2]
    for k in range(m):
        outs[k][pieces_rows:, :] = jnp.full((TAG, LANES), far[k][1], jnp.int32).astype(
            jnp.bfloat16
        )
        code_ref[k * TAG : (k + 1) * TAG, :] = jnp.full(
            (TAG, LANES), near[k][1], jnp.int32
        ).astype(jnp.bfloat16)
    mine = jnp.concatenate([ids(far[k][0], start, rows)[:, :1] for k in range(m)], axis=0)
    get_map.wait()
    merge_rows(
        map_ref[...] == mine,
        tok_ref,
        [(outs[k], rows) for k in range(m)],
        pieces,
        lambda c: strips[c].wait(),
    )
    at = 0
    for message in MESSAGES[1:]:
        ((other, start, rows),) = message
        for k in range(m):
            ids_ref[at : at + rows, :] = ids((far if other else near)[k][0], start, rows)
            at += rows


def later_merge_kernel(m, tok_ref, map_ref, ids_ref, code_ref, *outs):
    pieces = tok_ref.shape[1] // LANES
    at = 0
    for i, message in enumerate(MESSAGES[1:]):
        ((other, start, rows),) = message
        hot = map_ref[...] == ids_ref[at : at + m * rows, :1]
        spots = [(outs[i * m + k], rows) for k in range(m)]
        merge_rows(hot, tok_ref, spots, pieces, lambda c: None)
        if start == 0:
            for k in range(m):
                outs[i * m + k][pieces * rows :, :] = code_ref[k * TAG : (k + 1) * TAG, :]
        at += m * rows


def pad(m):
    return -(-m // TAG) * TAG


def is_slot(tag, s):
    return tag[0:1, :].astype(jnp.float32) == float(s)


def masks_of(tags, rows):
    return [[jnp.broadcast_to(is_slot(tag, s), (rows, LANES)) for s in range(OWN)] for tag in tags]


def gather_kernel(m, rows, tagged, *refs):
    blocks = refs[:m]
    if tagged:
        (out_ref,) = refs[m:]
        size = out_ref.shape[0] - pad(m)
        for k in range(m):
            out_ref[size + k : size + k + 1, :] = blocks[k][size // OWN : size // OWN + 1, :]
        tags = [blocks[k][size // OWN : size // OWN + TAG, :] for k in range(m)]
    else:
        known_ref, out_ref = refs[m:]
        size = out_ref.shape[0]
        first = known_ref.shape[0] - pad(m)
        tags = [known_ref[first + k : first + k + 1, :] for k in range(m)]
    masks = masks_of(tags, rows)
    for h in range(0, size // OWN, rows):
        pick = [jnp.zeros((rows, LANES), jnp.bfloat16)] * OWN
        for k in range(m):
            block = blocks[k][h : h + rows, :]
            pick = [jnp.where(masks[k][s], block, pick[s]) for s in range(OWN)]
        for s in range(OWN):
            out_ref[s * (size // OWN) + h : s * (size // OWN) + h + rows, :] = pick[s]


def project_kernel(m, rows, tagged, wk_ref, wv_ref, cross_ref, *refs):
    blocks, refs = refs[:m], refs[m:]
    if tagged:
        x_ref, kv_ref, tag_ref = refs
    else:
        tag_ref, x_ref, kv_ref = refs
    pieces = x_ref.shape[1] // LANES
    size = pieces * rows
    if tagged:
        for k in range(m):
            tag_ref[k] = blocks[k][size : size + TAG, :]
    masks = masks_of([tag_ref[k] for k in range(m)], rows)
    for h in range(pieces):
        pick = [jnp.zeros((rows, LANES), jnp.bfloat16)] * OWN
        for k in range(m):
            block = blocks[k][h * rows : (h + 1) * rows, :]
            pick = [jnp.where(masks[k][s], block, pick[s]) for s in range(OWN)]
        for s in range(OWN):
            other = cross_ref[s * size + h * rows : s * size + (h + 1) * rows, :]
            x_ref[s * rows : (s + 1) * rows, h * LANES : (h + 1) * LANES] = pick[s] + other
    x = x_ref[...]
    width = wk_ref.shape[1]

    def mul(w):
        return jnp.dot(x, w[...], preferred_element_type=jnp.float32).astype(jnp.bfloat16)

    kv_ref[:, :width] = mul(wk_ref)
    kv_ref[:, width:] = mul(wv_ref)


def query_kernel(wq_ref, *refs):
    xs, (q_ref,) = refs[:-1], refs[-1:]
    x = jnp.concatenate(
        [
            xs[c][s * rows : (s + 1) * rows, :]
            for s in range(OWN)
            for c, (_, rows) in enumerate(PARTS)
        ],
        axis=0,
    )
    q = jnp.dot(x, wq_ref[...], preferred_element_type=jnp.float32).astype(jnp.bfloat16)
    q = q * jnp.bfloat16(1.0 / math.sqrt(HD))
    low = lax.broadcasted_iota(jnp.int32, (BLK, LANES), 1) < HD
    zero = jnp.zeros((BLK, LANES), jnp.bfloat16)
    for s in range(OWN):
        for h in range(0, q.shape[1], LANES):
            piece = q[s * BLK : (s + 1) * BLK, h : h + LANES]
            at = 2 * s * BLK
            q_ref[at : at + BLK, h : h + LANES] = jnp.where(low, piece, zero)
            q_ref[at + BLK : at + 2 * BLK, h : h + LANES] = jnp.where(low, zero, piece)


def attend_kernel(m, n_col, tag_ref, bias_ref, q_ref, *refs):
    refs = list(refs)
    kvs, refs = refs[: len(PARTS) * n_col], refs[len(PARTS) * n_col :]
    outs, (back_ref, head_ref) = refs[:m], refs[m:]
    width = q_ref.shape[1]
    low = lax.broadcasted_iota(jnp.int32, (BLK, LANES), 1) < HD
    zero = jnp.zeros((BLK, LANES), jnp.bfloat16)
    keys = bias_ref.shape[1]
    bias = jnp.concatenate(
        [jnp.broadcast_to(bias_ref[s : s + 1, :], (2 * BLK, keys)) for s in range(OWN)], axis=0
    )
    for h in range(0, width, LANES):
        key = jnp.concatenate([kv[:, h : h + LANES] for kv in kvs], axis=0)
        value = jnp.concatenate([kv[:, width + h : width + h + LANES] for kv in kvs], axis=0)
        score = lax.dot_general(
            q_ref[:, h : h + LANES],
            key,
            (((1,), (1,)), ((), ())),
            preferred_element_type=jnp.float32,
        )
        score = score + bias
        p = jnp.exp(score - jnp.max(score, axis=1, keepdims=True))
        total = jnp.sum(p, axis=1, keepdims=True)
        o = jnp.dot(p.astype(jnp.bfloat16), value, preferred_element_type=jnp.float32)
        o = (o * (1.0 / total)).astype(jnp.bfloat16)
        for s in range(OWN):
            at = 2 * s * BLK
            head_ref[s, :, h : h + LANES] = jnp.where(
                low, o[at : at + BLK], o[at + BLK : at + 2 * BLK]
            )
    for s in range(OWN):
        back_ref[s * BLK : (s + 1) * BLK, :] = head_ref[s]
    masks = masks_of([tag_ref[k] for k in range(m)], BLK)
    for k in range(m):
        for h in range(0, width, LANES):
            pick = zero
            for s in range(OWN):
                pick = jnp.where(masks[k][s], head_ref[s, :, h : h + LANES], pick)
            outs[k][:, h : h + LANES] = pick


def relay_kernel(m, known_ref, back_ref, *outs):
    rows, width = outs[0].shape
    first = known_ref.shape[0] - pad(m)
    masks = masks_of([known_ref[first + k : first + k + 1, :] for k in range(m)], rows)
    zero = jnp.zeros((rows, LANES), jnp.bfloat16)
    for k in range(m):
        for h in range(0, width, LANES):
            pick = zero
            for s in range(OWN):
                block = back_ref[s * rows : (s + 1) * rows, h : h + LANES]
                pick = jnp.where(masks[k][s], block, pick)
            outs[k][:, h : h + LANES] = pick


def spread_kernel(n, n_col, slots, map_ref, owner_ref, near_ref, out_ref, bias_ref):
    me = lax.axis_index("row")
    my_col = lax.axis_index("col")
    near = near_ref.shape[1]
    at = 0
    for _, rows in PARTS:
        for k in range(n_col):
            for t in range(OWN):
                cand = partner(my_col, k, n_col, True) * OWN + t
                for s in range(OWN):
                    hit = near_ref[s, 0] == cand
                    for j in range(1, near):
                        hit = hit | (near_ref[s, j] == cand)
                    bias_ref[s : s + 1, at : at + rows] = jnp.full(
                        (1, rows), jnp.where(hit, 0.0, -1e30), jnp.float32
                    )
                at += rows
    mm = map_ref[...]
    block = mm // BLK
    target = mm % BLK
    for k in range(n):
        slot, _ = slot_of(owner_ref, peer(me, k, n), slots)
        target = target + jnp.where((block == slot) & (slot >= 0), k * BLK, 0)
    toks = mm.shape[1]
    for k0 in range(0, n * BLK, LANES):
        ids = lax.broadcasted_iota(jnp.int32, (LANES, toks), 0) + k0
        hot = (ids == target).astype(jnp.float32)
        out_ref[:, k0 : k0 + LANES] = jnp.transpose(hot).astype(jnp.bfloat16)


def part_kernel(m, spread_ref, *refs):
    blocks, (out_ref, all_ref) = refs[:m], refs[m:]
    for k in range(m):
        all_ref[k * BLK : (k + 1) * BLK, :] = blocks[k][...]
    out_ref[...] = jnp.dot(
        spread_ref[:, : m * BLK], all_ref[...], preferred_element_type=jnp.float32
    ).astype(out_ref.dtype)


def return_kernel(m, spread_ref, part_ref, *refs):
    blocks, (out_hbm, all_ref, out_ref, sems) = refs[:-4], refs[-4:]
    for k in range(m):
        all_ref[k * BLK : (k + 1) * BLK, :] = blocks[k][...]
    step = out_ref.shape[0] // RETURN_STEPS
    copies = []
    for i in range(RETURN_STEPS):
        rows = slice(i * step, (i + 1) * step)
        far = jnp.dot(
            spread_ref[rows, m * BLK :], all_ref[...], preferred_element_type=jnp.float32
        )
        out_ref[rows, :] = part_ref[rows, :] + far.astype(out_ref.dtype)
        copies.append(
            pltpu.make_async_copy(out_ref.at[rows, :], out_hbm.at[rows, :], sems.at[i])
        )
        copies[-1].start()
    for copy in copies:
        copy.wait()


def on_device(tokens, merge_map, block_owner, neighbours, w_query, w_key, w_value):
    n = lax.axis_size("row")
    n_col = lax.axis_size("col")
    toks, width = tokens.shape
    heads = w_query.shape[1]
    slots = block_owner.shape[1]
    bf16 = jnp.bfloat16

    def shape(*s, dtype=bf16):
        return jax.ShapeDtypeStruct(s, dtype)

    mm = pltpu.with_memory_space_constraint(merge_map.reshape(1, toks), pltpu.HBM)
    tokens = pltpu.with_memory_space_constraint(tokens, pltpu.HBM)
    block_owner = pltpu.with_memory_space_constraint(block_owner, pltpu.HBM)
    neighbours = pltpu.with_memory_space_constraint(neighbours, pltpu.HBM)
    m = n // 2
    pieces = width // LANES

    def message_shapes(message):
        size = rows_of(message) * pieces + TAG * any(part[1] == 0 for part in message)
        return [shape(size, LANES)] * m

    rest = sum(rows_of(message) for message in MESSAGES[1:]) * m
    *far0, toks_in, map_in, ids, codes = pl.pallas_call(
        functools.partial(first_merge_kernel, n, slots),
        out_shape=message_shapes(MESSAGES[0])
        + [
            shape(toks, width),
            shape(1, toks, dtype=jnp.int32),
            shape(rest, LANES, dtype=jnp.int32),
            shape(m * TAG, LANES),
        ],
        in_specs=[HBM] * 3,
        out_specs=[VMEM] * (m + 4),
        scratch_shapes=[
            pltpu.SMEM(block_owner.shape, jnp.int32),
            pltpu.SemaphoreType.DMA((2 + pieces // STRIP,)),
        ],
        compiler_params=PARAMS,
        cost_estimate=cost(2),
        name="merge",
    )(tokens, mm, block_owner)
    far0 = rounds(far0, "row", n, inner)
    outs = pl.pallas_call(
        functools.partial(later_merge_kernel, m),
        out_shape=[x for message in MESSAGES[1:] for x in message_shapes(message)],
        in_specs=[VMEM] * 4,
        out_specs=[VMEM] * (3 * m),
        compiler_params=PARAMS,
        cost_estimate=cost(2),
        name="merge_rest",
    )(toks_in, map_in, ids, codes)
    far1, own0, own1 = outs[:m], outs[m : 2 * m], outs[2 * m :]

    def gather(c, blocks, *known):
        rows = PARTS[c][1]
        out = pl.pallas_call(
            functools.partial(gather_kernel, m, rows, not known),
            out_shape=shape(OWN * rows * pieces + (0 if known else pad(m)), LANES),
            in_specs=[VMEM] * (m + len(known)),
            out_specs=VMEM,
            compiler_params=PARAMS,
            cost_estimate=cost(0.5),
            name="gather",
        )(*blocks, *known)
        return out, lax.ppermute(out, "row", [(i, across(i, n)) for i in range(n)])

    def project(c, cross, blocks, *tags):
        rows = PARTS[c][1]
        out = pl.pallas_call(
            functools.partial(project_kernel, m, rows, not tags),
            out_shape=[shape(OWN * rows, width), shape(OWN * rows, 2 * heads)]
            + [shape(m, TAG, LANES)] * (not tags),
            in_specs=[VMEM] * (3 + m + len(tags)),
            out_specs=[VMEM] * (2 + (not tags)),
            compiler_params=PARAMS,
            cost_estimate=cost(1),
            name="project",
        )(w_key, w_value, cross, *blocks, *tags)
        return out, rounds([out[1]] * n_col, "col", n_col, partner)

    far1 = rounds(far1, "row", n, inner)
    known, cross0 = gather(0, far0)
    own0 = rounds(own0, "row", n, inner)
    own1 = rounds(own1, "row", n, inner)
    _, cross1 = gather(1, far1, known)
    (x0, _, tags), kv0 = project(0, cross0, own0)
    (x1, _), kv1 = project(1, cross1, own1, tags)
    kvs = kv0 + kv1
    queries = pl.pallas_call(
        query_kernel,
        out_shape=shape(OWN * 2 * BLK, heads),
        in_specs=[VMEM] * 3,
        out_specs=VMEM,
        compiler_params=PARAMS,
        cost_estimate=cost(1),
        name="query",
    )(w_query, x0, x1)
    spread, bias = pl.pallas_call(
        functools.partial(spread_kernel, n, n_col, slots),
        out_shape=[
            shape(toks, n * BLK),
            shape(TAG, n_col * OWN * BLK, dtype=jnp.float32),
        ],
        in_specs=[VMEM, SMEM, SMEM],
        out_specs=[VMEM, VMEM],
        compiler_params=PARAMS,
        cost_estimate=cost(2),
        name="spread",
    )(map_in, block_owner, neighbours)
    outs = pl.pallas_call(
        functools.partial(attend_kernel, m, n_col),
        out_shape=[shape(BLK, heads)] * m + [shape(OWN * BLK, heads)],
        in_specs=[VMEM] * (3 + len(kvs)),
        out_specs=[VMEM] * (m + 1),
        scratch_shapes=[pltpu.VMEM((OWN, BLK, heads), bf16)],
        compiler_params=PARAMS,
        cost_estimate=cost(3),
        name="attend",
    )(tags, bias, queries, *kvs)
    back = lax.ppermute(outs[m], "row", [(i, across(i, n)) for i in range(n)])
    to_sender = functools.partial(inner, back=True)
    homes = rounds(outs[:m], "row", n, to_sender)
    relayed = pl.pallas_call(
        functools.partial(relay_kernel, m),
        out_shape=[shape(BLK, heads)] * m,
        in_specs=[VMEM] * 2,
        out_specs=[VMEM] * m,
        compiler_params=PARAMS,
        cost_estimate=cost(0.5),
        name="relay",
    )(known, back)
    relayed = rounds(relayed, "row", n, to_sender)
    part = pl.pallas_call(
        functools.partial(part_kernel, m),
        out_shape=shape(toks, heads),
        in_specs=[VMEM] * (1 + m),
        out_specs=VMEM,
        scratch_shapes=[pltpu.VMEM((m * BLK, heads), bf16)],
        compiler_params=PARAMS,
        cost_estimate=cost(1),
        name="part",
    )(spread, *homes)
    return pl.pallas_call(
        functools.partial(return_kernel, m),
        out_shape=shape(toks, heads),
        in_specs=[VMEM] * (2 + m),
        out_specs=HBM,
        scratch_shapes=[
            pltpu.VMEM((m * BLK, heads), bf16),
            pltpu.VMEM((toks, heads), bf16),
            pltpu.SemaphoreType.DMA((RETURN_STEPS,)),
        ],
        compiler_params=PARAMS,
        cost_estimate=cost(2),
        name="give_back",
    )(spread, part, *relayed)


def solution(mesh):
    in_specs = (
        P(("row", "col"), None),
        P(("row", "col")),
        P(("row", "col"), None),
        P(("row", "col"), None),
        P(),
        P(),
        P(),
    )
    out_specs = P(("row", "col"), None)

    return jax.shard_map(
        on_device, mesh=mesh, in_specs=in_specs, out_specs=out_specs, check_vma=False
    )
```

```python
import functools
import math

import jax
import jax.numpy as jnp
from jax import lax
from jax.experimental import pallas as pl
from jax.experimental.pallas import tpu as pltpu
from jax.sharding import PartitionSpec as P


HD = 64
BLK = 64
OWN = 2
LANES = 128
TAG = 8
STRIP = 8
RETURN_STEPS = 4


VMEM = pl.BlockSpec(memory_space=pltpu.VMEM)
SMEM = pl.BlockSpec(memory_space=pltpu.SMEM)
HBM = pl.BlockSpec(memory_space=pltpu.HBM)
PARAMS = pltpu.CompilerParams(vmem_limit_bytes=16 << 20)


def partner(i, k, n, back=False):
    if n & (n - 1) == 0:
        return i ^ k
    return (i - k + n) % n if back else (i + k) % n


def inner(i, k, n, back=False):
    m = n // 2
    side = (i >= m) * m
    return side + partner(i - side, k, m, back)


def across(i, n):
    m = n // 2
    return i + m - (i >= m) * n


def peer(i, k, n, back=False):
    m = n // 2
    return inner(i, k, n, back) if k < m else across(inner(i, k - m, n, back), n)


def order(n, sign=1):
    return sorted(range(1, n), key=lambda k: (-(k.bit_length() - 1 if k > 1 else 0), sign * k))


def rounds(x, axis, n, to):
    out = list(x)
    for k in order(len(x)):
        out[k] = lax.ppermute(x[k], axis, [(i, to(i, k, n)) for i in range(n)])
    return out


def cost(us):
    return pl.CostEstimate(
        flops=int(us * 8e8), bytes_accessed=int(us * 2e6), transcendentals=0
    )


FIRST = (0, BLK // 2)
SECOND = (BLK // 2, BLK - BLK // 2)
PARTS = (FIRST, SECOND)
MESSAGES = (
    ((True, *FIRST),),
    ((True, *SECOND),),
    ((False, *FIRST),),
    ((False, *SECOND),),
)


def slot_of(owner_ref, row, slots):
    slot = jnp.int32(-1)
    code = jnp.int32(-1)
    for b in range(slots):
        o = owner_ref[0, b]
        hit = (o >= 0) & (o // OWN == row)
        slot = jnp.where(hit, b, slot)
        code = jnp.where(hit, o % OWN, code)
    return slot, code


def rows_of(message):
    return sum(part[2] for part in message)


def merge_rows(hot, tok_ref, spots, pieces, ready):
    hot = hot.astype(jnp.float32)
    scale = 1.0 / jnp.maximum(jnp.sum(hot, axis=1, keepdims=True), 1.0)
    hot = hot.astype(jnp.bfloat16)
    for c in range(0, pieces, STRIP):
        ready(c // STRIP)
        columns = tok_ref[:, c * LANES : (c + STRIP) * LANES]
        sums = jnp.dot(hot, columns, preferred_element_type=jnp.float32)
        merged = (sums * scale).astype(jnp.bfloat16)
        row = 0
        for ref, rows in spots:
            for h in range(STRIP):
                at = (c + h) * rows
                ref[at : at + rows, :] = merged[row : row + rows, h * LANES : (h + 1) * LANES]
            row += rows


def first_merge_kernel(n, slots, tok_hbm, map_hbm, owner_hbm, *refs):
    m = n // 2
    outs = refs[:m]
    tok_ref, map_ref, ids_ref, code_ref, owner_ref, sems = refs[m:]
    _, width = tok_ref.shape
    pieces = width // LANES
    strips = [
        pltpu.make_async_copy(
            tok_hbm.at[:, c * LANES : (c + STRIP) * LANES],
            tok_ref.at[:, c * LANES : (c + STRIP) * LANES],
            sems.at[2 + c // STRIP],
        )
        for c in range(0, pieces, STRIP)
    ]
    get_owner = pltpu.make_async_copy(owner_hbm, owner_ref, sems.at[0])
    get_map = pltpu.make_async_copy(map_hbm, map_ref, sems.at[1])
    for copy in (get_owner, get_map, *strips):
        copy.start()
    me = lax.axis_index("row")
    get_owner.wait()
    to = [inner(me, k, n) for k in range(m)]
    near = [slot_of(owner_ref, to[k], slots) for k in range(m)]
    far = [slot_of(owner_ref, across(to[k], n), slots) for k in range(m)]

    def ids(slot, start, rows):
        base = jnp.where(slot >= 0, slot * BLK + start, -BLK)
        return lax.broadcasted_iota(jnp.int32, (rows, LANES), 0) + base

    (_, start, rows), pieces_rows = MESSAGES[0][0], pieces * MESSAGES[0][0][2]
    for k in range(m):
        outs[k][pieces_rows:, :] = jnp.full((TAG, LANES), far[k][1], jnp.int32).astype(
            jnp.bfloat16
        )
        code_ref[k * TAG : (k + 1) * TAG, :] = jnp.full(
            (TAG, LANES), near[k][1], jnp.int32
        ).astype(jnp.bfloat16)
    mine = jnp.concatenate([ids(far[k][0], start, rows)[:, :1] for k in range(m)], axis=0)
    get_map.wait()
    merge_rows(
        map_ref[...] == mine,
        tok_ref,
        [(outs[k], rows) for k in range(m)],
        pieces,
        lambda c: strips[c].wait(),
    )
    at = 0
    for message in MESSAGES[1:]:
        ((other, start, rows),) = message
        for k in range(m):
            ids_ref[at : at + rows, :] = ids((far if other else near)[k][0], start, rows)
            at += rows


def later_merge_kernel(m, tok_ref, map_ref, ids_ref, code_ref, *outs):
    pieces = tok_ref.shape[1] // LANES
    at = 0
    for i, message in enumerate(MESSAGES[1:]):
        ((other, start, rows),) = message
        hot = map_ref[...] == ids_ref[at : at + m * rows, :1]
        spots = [(outs[i * m + k], rows) for k in range(m)]
        merge_rows(hot, tok_ref, spots, pieces, lambda c: None)
        if start == 0:
            for k in range(m):
                outs[i * m + k][pieces * rows :, :] = code_ref[k * TAG : (k + 1) * TAG, :]
        at += m * rows


def pad(m):
    return -(-m // TAG) * TAG


def is_slot(tag, s):
    return tag[0:1, :].astype(jnp.float32) == float(s)


def masks_of(tags, rows):
    return [[jnp.broadcast_to(is_slot(tag, s), (rows, LANES)) for s in range(OWN)] for tag in tags]


def gather_kernel(m, rows, tagged, *refs):
    blocks = refs[:m]
    if tagged:
        (out_ref,) = refs[m:]
        size = out_ref.shape[0] - pad(m)
        for k in range(m):
            out_ref[size + k : size + k + 1, :] = blocks[k][size // OWN : size // OWN + 1, :]
        tags = [blocks[k][size // OWN : size // OWN + TAG, :] for k in range(m)]
    else:
        known_ref, out_ref = refs[m:]
        size = out_ref.shape[0]
        first = known_ref.shape[0] - pad(m)
        tags = [known_ref[first + k : first + k + 1, :] for k in range(m)]
    masks = masks_of(tags, rows)
    for h in range(0, size // OWN, rows):
        pick = [jnp.zeros((rows, LANES), jnp.bfloat16)] * OWN
        for k in range(m):
            block = blocks[k][h : h + rows, :]
            pick = [jnp.where(masks[k][s], block, pick[s]) for s in range(OWN)]
        for s in range(OWN):
            out_ref[s * (size // OWN) + h : s * (size // OWN) + h + rows, :] = pick[s]


def project_kernel(m, rows, tagged, wk_ref, wv_ref, cross_ref, *refs):
    blocks, refs = refs[:m], refs[m:]
    if tagged:
        x_ref, kv_ref, tag_ref = refs
    else:
        tag_ref, x_ref, kv_ref = refs
    pieces = x_ref.shape[1] // LANES
    size = pieces * rows
    if tagged:
        for k in range(m):
            tag_ref[k] = blocks[k][size : size + TAG, :]
    masks = masks_of([tag_ref[k] for k in range(m)], rows)
    for h in range(pieces):
        pick = [jnp.zeros((rows, LANES), jnp.bfloat16)] * OWN
        for k in range(m):
            block = blocks[k][h * rows : (h + 1) * rows, :]
            pick = [jnp.where(masks[k][s], block, pick[s]) for s in range(OWN)]
        for s in range(OWN):
            other = cross_ref[s * size + h * rows : s * size + (h + 1) * rows, :]
            x_ref[s * rows : (s + 1) * rows, h * LANES : (h + 1) * LANES] = pick[s] + other
    x = x_ref[...]
    width = wk_ref.shape[1]

    def mul(w):
        return jnp.dot(x, w[...], preferred_element_type=jnp.float32).astype(jnp.bfloat16)

    kv_ref[:, :width] = mul(wk_ref)
    kv_ref[:, width:] = mul(wv_ref)


def query_kernel(wq_ref, *refs):
    xs, (q_ref,) = refs[:-1], refs[-1:]
    x = jnp.concatenate(
        [
            xs[c][s * rows : (s + 1) * rows, :]
            for s in range(OWN)
            for c, (_, rows) in enumerate(PARTS)
        ],
        axis=0,
    )
    q = jnp.dot(x, wq_ref[...], preferred_element_type=jnp.float32).astype(jnp.bfloat16)
    q = q * jnp.bfloat16(1.0 / math.sqrt(HD))
    low = lax.broadcasted_iota(jnp.int32, (BLK, LANES), 1) < HD
    zero = jnp.zeros((BLK, LANES), jnp.bfloat16)
    for s in range(OWN):
        for h in range(0, q.shape[1], LANES):
            piece = q[s * BLK : (s + 1) * BLK, h : h + LANES]
            at = 2 * s * BLK
            q_ref[at : at + BLK, h : h + LANES] = jnp.where(low, piece, zero)
            q_ref[at + BLK : at + 2 * BLK, h : h + LANES] = jnp.where(low, zero, piece)


def attend_kernel(n_col, bias_ref, q_ref, *refs):
    refs = list(refs)
    kvs, refs = refs[: len(PARTS) * n_col], refs[len(PARTS) * n_col :]
    (back_ref,) = refs
    width = q_ref.shape[1]
    low = lax.broadcasted_iota(jnp.int32, (BLK, LANES), 1) < HD
    keys = bias_ref.shape[1]
    bias = jnp.concatenate(
        [jnp.broadcast_to(bias_ref[s : s + 1, :], (2 * BLK, keys)) for s in range(OWN)], axis=0
    )
    for h in range(0, width, LANES):
        key = jnp.concatenate([kv[:, h : h + LANES] for kv in kvs], axis=0)
        value = jnp.concatenate([kv[:, width + h : width + h + LANES] for kv in kvs], axis=0)
        score = lax.dot_general(
            q_ref[:, h : h + LANES],
            key,
            (((1,), (1,)), ((), ())),
            preferred_element_type=jnp.float32,
        )
        score = score + bias
        p = jnp.exp(score - jnp.max(score, axis=1, keepdims=True))
        total = jnp.sum(p, axis=1, keepdims=True)
        o = jnp.dot(p.astype(jnp.bfloat16), value, preferred_element_type=jnp.float32)
        o = (o * (1.0 / total)).astype(jnp.bfloat16)
        for s in range(OWN):
            at = 2 * s * BLK
            back_ref[s * BLK : (s + 1) * BLK, h : h + LANES] = jnp.where(
                low, o[at : at + BLK], o[at + BLK : at + 2 * BLK]
            )


def hand_out(tags, back_ref, outs):
    rows, width = outs[0].shape
    masks = masks_of(tags, rows)
    zero = jnp.zeros((rows, LANES), jnp.bfloat16)
    for k in range(len(outs)):
        for h in range(0, width, LANES):
            pick = zero
            for s in range(OWN):
                block = back_ref[s * rows : (s + 1) * rows, h : h + LANES]
                pick = jnp.where(masks[k][s], block, pick)
            outs[k][:, h : h + LANES] = pick


def reply_kernel(tag_ref, back_ref, *outs):
    hand_out([tag_ref[k] for k in range(len(outs))], back_ref, outs)


def relay_kernel(known_ref, back_ref, *outs):
    m = len(outs)
    first = known_ref.shape[0] - pad(m)
    hand_out([known_ref[first + k : first + k + 1, :] for k in range(m)], back_ref, outs)


def spread_kernel(n, n_col, slots, map_ref, owner_ref, near_ref, out_ref, bias_ref):
    me = lax.axis_index("row")
    my_col = lax.axis_index("col")
    near = near_ref.shape[1]
    at = 0
    for _, rows in PARTS:
        for k in range(n_col):
            for t in range(OWN):
                cand = partner(my_col, k, n_col, True) * OWN + t
                for s in range(OWN):
                    hit = near_ref[s, 0] == cand
                    for j in range(1, near):
                        hit = hit | (near_ref[s, j] == cand)
                    bias_ref[s : s + 1, at : at + rows] = jnp.full(
                        (1, rows), jnp.where(hit, 0.0, -1e30), jnp.float32
                    )
                at += rows
    mm = map_ref[...]
    block = mm // BLK
    target = mm % BLK
    for k in range(n):
        slot, _ = slot_of(owner_ref, peer(me, k, n), slots)
        target = target + jnp.where((block == slot) & (slot >= 0), k * BLK, 0)
    toks = mm.shape[1]
    for k0 in range(0, n * BLK, LANES):
        ids = lax.broadcasted_iota(jnp.int32, (LANES, toks), 0) + k0
        hot = (ids == target).astype(jnp.float32)
        out_ref[:, k0 : k0 + LANES] = jnp.transpose(hot).astype(jnp.bfloat16)


def part_kernel(m, spread_ref, *refs):
    blocks, (out_ref, all_ref) = refs[:m], refs[m:]
    for k in range(m):
        all_ref[k * BLK : (k + 1) * BLK, :] = blocks[k][...]
    out_ref[...] = jnp.dot(
        spread_ref[:, : m * BLK], all_ref[...], preferred_element_type=jnp.float32
    ).astype(out_ref.dtype)


def return_kernel(m, spread_ref, part_ref, *refs):
    blocks, (out_hbm, all_ref, out_ref, sems) = refs[:-4], refs[-4:]
    for k in range(m):
        all_ref[k * BLK : (k + 1) * BLK, :] = blocks[k][...]
    step = out_ref.shape[0] // RETURN_STEPS
    copies = []
    for i in range(RETURN_STEPS):
        rows = slice(i * step, (i + 1) * step)
        far = jnp.dot(
            spread_ref[rows, m * BLK :], all_ref[...], preferred_element_type=jnp.float32
        )
        out_ref[rows, :] = part_ref[rows, :] + far.astype(out_ref.dtype)
        copies.append(
            pltpu.make_async_copy(out_ref.at[rows, :], out_hbm.at[rows, :], sems.at[i])
        )
        copies[-1].start()
    for copy in copies:
        copy.wait()


def on_device(tokens, merge_map, block_owner, neighbours, w_query, w_key, w_value):
    n = lax.axis_size("row")
    n_col = lax.axis_size("col")
    toks, width = tokens.shape
    heads = w_query.shape[1]
    slots = block_owner.shape[1]
    bf16 = jnp.bfloat16

    def shape(*s, dtype=bf16):
        return jax.ShapeDtypeStruct(s, dtype)

    mm = pltpu.with_memory_space_constraint(merge_map.reshape(1, toks), pltpu.HBM)
    tokens = pltpu.with_memory_space_constraint(tokens, pltpu.HBM)
    block_owner = pltpu.with_memory_space_constraint(block_owner, pltpu.HBM)
    neighbours = pltpu.with_memory_space_constraint(neighbours, pltpu.HBM)
    m = n // 2
    pieces = width // LANES

    def message_shapes(message):
        size = rows_of(message) * pieces + TAG * any(part[1] == 0 for part in message)
        return [shape(size, LANES)] * m

    rest = sum(rows_of(message) for message in MESSAGES[1:]) * m
    *far0, toks_in, map_in, ids, codes = pl.pallas_call(
        functools.partial(first_merge_kernel, n, slots),
        out_shape=message_shapes(MESSAGES[0])
        + [
            shape(toks, width),
            shape(1, toks, dtype=jnp.int32),
            shape(rest, LANES, dtype=jnp.int32),
            shape(m * TAG, LANES),
        ],
        in_specs=[HBM] * 3,
        out_specs=[VMEM] * (m + 4),
        scratch_shapes=[
            pltpu.SMEM(block_owner.shape, jnp.int32),
            pltpu.SemaphoreType.DMA((2 + pieces // STRIP,)),
        ],
        compiler_params=PARAMS,
        cost_estimate=cost(2),
        name="merge",
    )(tokens, mm, block_owner)
    far0 = rounds(far0, "row", n, inner)
    outs = pl.pallas_call(
        functools.partial(later_merge_kernel, m),
        out_shape=[x for message in MESSAGES[1:] for x in message_shapes(message)],
        in_specs=[VMEM] * 4,
        out_specs=[VMEM] * (3 * m),
        compiler_params=PARAMS,
        cost_estimate=cost(2),
        name="merge_rest",
    )(toks_in, map_in, ids, codes)
    far1, own0, own1 = outs[:m], outs[m : 2 * m], outs[2 * m :]

    def gather(c, blocks, *known):
        rows = PARTS[c][1]
        out = pl.pallas_call(
            functools.partial(gather_kernel, m, rows, not known),
            out_shape=shape(OWN * rows * pieces + (0 if known else pad(m)), LANES),
            in_specs=[VMEM] * (m + len(known)),
            out_specs=VMEM,
            compiler_params=PARAMS,
            cost_estimate=cost(0.5),
            name="gather",
        )(*blocks, *known)
        return out, lax.ppermute(out, "row", [(i, across(i, n)) for i in range(n)])

    def project(c, cross, blocks, *tags):
        rows = PARTS[c][1]
        out = pl.pallas_call(
            functools.partial(project_kernel, m, rows, not tags),
            out_shape=[shape(OWN * rows, width), shape(OWN * rows, 2 * heads)]
            + [shape(m, TAG, LANES)] * (not tags),
            in_specs=[VMEM] * (3 + m + len(tags)),
            out_specs=[VMEM] * (2 + (not tags)),
            compiler_params=PARAMS,
            cost_estimate=cost(1),
            name="project",
        )(w_key, w_value, cross, *blocks, *tags)
        return out, rounds([out[1]] * n_col, "col", n_col, partner)

    far1 = rounds(far1, "row", n, inner)
    known, cross0 = gather(0, far0)
    own0 = rounds(own0, "row", n, inner)
    own1 = rounds(own1, "row", n, inner)
    _, cross1 = gather(1, far1, known)
    (x0, _, tags), kv0 = project(0, cross0, own0)
    (x1, _), kv1 = project(1, cross1, own1, tags)
    kvs = kv0 + kv1
    queries = pl.pallas_call(
        query_kernel,
        out_shape=shape(OWN * 2 * BLK, heads),
        in_specs=[VMEM] * 3,
        out_specs=VMEM,
        compiler_params=PARAMS,
        cost_estimate=cost(1),
        name="query",
    )(w_query, x0, x1)
    spread, bias = pl.pallas_call(
        functools.partial(spread_kernel, n, n_col, slots),
        out_shape=[
            shape(toks, n * BLK),
            shape(TAG, n_col * OWN * BLK, dtype=jnp.float32),
        ],
        in_specs=[VMEM, SMEM, SMEM],
        out_specs=[VMEM, VMEM],
        compiler_params=PARAMS,
        cost_estimate=cost(2),
        name="spread",
    )(map_in, block_owner, neighbours)
    mine = pl.pallas_call(
        functools.partial(attend_kernel, n_col),
        out_shape=shape(OWN * BLK, heads),
        in_specs=[VMEM] * (2 + len(kvs)),
        out_specs=VMEM,
        compiler_params=PARAMS,
        cost_estimate=cost(3),
        name="attend",
    )(bias, queries, *kvs)

    def to_tiles(kernel, known, blocks):
        return pl.pallas_call(
            kernel,
            out_shape=[shape(BLK, heads)] * m,
            in_specs=[VMEM] * 2,
            out_specs=[VMEM] * m,
            compiler_params=PARAMS,
            cost_estimate=cost(0.5),
        )(known, blocks)

    back = lax.ppermute(mine, "row", [(i, across(i, n)) for i in range(n)])
    to_sender = functools.partial(inner, back=True)
    homes = rounds(to_tiles(reply_kernel, tags, mine), "row", n, to_sender)
    relayed = to_tiles(relay_kernel, known, back)
    relayed = rounds(relayed, "row", n, to_sender)
    part = pl.pallas_call(
        functools.partial(part_kernel, m),
        out_shape=shape(toks, heads),
        in_specs=[VMEM] * (1 + m),
        out_specs=VMEM,
        scratch_shapes=[pltpu.VMEM((m * BLK, heads), bf16)],
        compiler_params=PARAMS,
        cost_estimate=cost(1),
        name="part",
    )(spread, *homes)
    return pl.pallas_call(
        functools.partial(return_kernel, m),
        out_shape=shape(toks, heads),
        in_specs=[VMEM] * (2 + m),
        out_specs=HBM,
        scratch_shapes=[
            pltpu.VMEM((m * BLK, heads), bf16),
            pltpu.VMEM((toks, heads), bf16),
            pltpu.SemaphoreType.DMA((RETURN_STEPS,)),
        ],
        compiler_params=PARAMS,
        cost_estimate=cost(2),
        name="give_back",
    )(spread, part, *relayed)


def solution(mesh):
    in_specs = (
        P(("row", "col"), None),
        P(("row", "col")),
        P(("row", "col"), None),
        P(("row", "col"), None),
        P(),
        P(),
        P(),
    )
    out_specs = P(("row", "col"), None)

    return jax.shard_map(
        on_device, mesh=mesh, in_specs=in_specs, out_specs=out_specs, check_vma=False
    )
```
